32 devices in a mesh: grp: 2 (over x), dp: 8 (over z, y), tp: 2 (over core).
Axes of the slice: x: 2, y: 2, z: 4, core: 2. Of those that a mesh axis runs over, the one named last changes fastest.
Arguments:
- frames: bfloat16 [2, 16, 128, 1280], P('grp', ('dp', 'tp')), may hold values from -12 to 12
- counts: int32 [16], P('dp'), may hold values from 0 to 1, as said below
- w_qkv: bfloat16 [2, 1280, 3840], P('grp'), may hold values from -0.18727069 to 0.18727069
- ln_gain: bfloat16 [2, 1280], P('grp'), may hold values from 0.5 to 1.5
- w_proj: bfloat16 [2, 5120, 8192], P('grp', 'dp', 'tp'), may hold values from -1.5931984 to 1.5931984
- rms_gain: bfloat16 [2, 8192], P('grp', 'tp'), may hold values from 0.5 to 1.5
- cotangent: bfloat16 [2, 512, 8192], P('grp', 'dp', 'tp'), may hold values from -6 to 6
Outputs:
- frame_grad: bfloat16 [2, 16, 128, 1280], P('grp', ('dp', 'tp'))
The draws below stay inside these ranges and needn't reach their ends.
Inputs may be any that keep to these rules, and one draw needn't show every extreme that they name: `counts`: some encoder device has all 1 frames live.
All inputs are finite; a program needn't handle non-finite values.
Results may differ from the reference program's by a relative error of at most 0.025.
Values may be sent and summed in bfloat16 or wider, within the bound.
No kernel may reach another device: no remote copies, remote signals or barrier semaphores. Data moves between devices by JAX's collectives and lax.ppermute only.
A program may use at most 128 MiB of HBM per device.

```python
import jax
import jax.numpy as jnp
from jax import lax

VIS = 1280
HEADS = 16
HDIM = 80
D = 8192
DM = 5120
P_SIZE = 128
FR_DEV = 1
TOKF = 32
FRAMES = 16
TOKENS = 512
N_GRP = 2
N_DP = 8
N_TP = 2


def draw_frames(key, part):
    key_base = jax.random.fold_in(key, 11)
    full_shape = (N_GRP, FRAMES, P_SIZE, VIS)
    return jnp.clip(jax.random.normal(key_base, full_shape, jnp.float32), -5.0, 5.0).astype(jnp.bfloat16)


def draw_w_qkv(key, part):
    key_main = jax.random.fold_in(key, 21)
    factor = VIS ** (-0.5)
    weights = jnp.clip(jax.random.normal(key_main, (N_GRP, VIS, 3 * VIS), jnp.float32), -5.0, 5.0) * factor
    return weights.astype(jnp.bfloat16)


def draw_w_proj(key, part):
    key_main = jax.random.fold_in(key, 31)
    key_scale = jax.random.fold_in(key, 32)
    weights = jnp.clip(jax.random.normal(key_main, (N_GRP, DM, D), jnp.float32), -4.0, 4.0) * DM ** (-0.5)
    column_index = lax.broadcasted_iota(jnp.int32, (D,), 0).astype(jnp.float32)
    column_ramp = jnp.exp(jnp.log(3.0) * column_index / D)
    spread = jnp.exp(jnp.log(10.0) * (jax.random.uniform(key_scale, (D,), jnp.float32) - 0.5))
    return (weights * (column_ramp * spread)[None, None, :]).astype(jnp.bfloat16)


def draw_counts(key, part):
    key_base = jax.random.fold_in(key, 41)
    key_full = jax.random.fold_in(key, 42)
    base_draw = jax.random.randint(key_base, (N_DP * N_TP,), 0, FR_DEV + 1)
    full_device = jax.random.randint(key_full, (), 0, N_DP * N_TP)
    device_index = jnp.arange(N_DP * N_TP, dtype=jnp.int32)
    return jnp.where(device_index == full_device, FR_DEV, base_draw).astype(jnp.int32)


def shard_levels(rng, dims, cuts, low, high):
    level = 1.0
    for dim, shards_of in cuts:
        heights = jax.random.uniform(jax.random.fold_in(jax.random.fold_in(rng, 6), dim), (shards_of,), jnp.float32, low / len(cuts), high / len(cuts))
        level = level * jnp.repeat(jnp.exp(heights), dims[dim] // shards_of).reshape((-1,) + (1,) * (len(dims) - 1 - dim))
    return level


def gaussian(own_key, extent, width, reach, cuts=(), kind=jnp.bfloat16):
    factor_of = shard_levels(own_key, extent, cuts, -0.22, 0.18) if cuts else 1.0
    result = jax.random.normal(own_key, extent, jnp.float32) * width * factor_of
    return jnp.minimum(jnp.maximum(result, -reach), reach).astype(kind)


def setup_inputs(seed: int = 0) -> dict:
    seeds = jax.random.split(jax.random.key(seed), 8)
    frames = draw_frames(jax.random.fold_in(seeds[7], 71), 0)
    counts = draw_counts(jax.random.fold_in(seeds[7], 71), 0)
    w_qkv = draw_w_qkv(jax.random.fold_in(seeds[7], 71), 0)
    ln_gain = jnp.clip(1.0 + 0.1 * jax.random.normal(seeds[3], (N_GRP, VIS), jnp.float32), 0.5, 1.5).astype(jnp.bfloat16)
    w_proj = draw_w_proj(jax.random.fold_in(seeds[7], 71), 0)
    rms_gain = jnp.clip(1.0 + 0.1 * jax.random.normal(seeds[5], (N_GRP, D), jnp.float32), 0.5, 1.5).astype(jnp.bfloat16)
    cotangent = gaussian(seeds[6], (N_GRP, TOKENS, D), 1.0, 6.0, ((0, 2), (1, 8), (2, 2)))
    return {"frames": frames, "counts": counts, "w_qkv": w_qkv, "ln_gain": ln_gain, "w_proj": w_proj, "rms_gain": rms_gain, "cotangent": cotangent}


def encoder_forward(frames, w_qkv, ln_gain):
    frame_count = frames.shape[0]
    length = frames.shape[1]
    vis_width = frames.shape[2]
    mixed_qkv = jnp.einsum('fpe,ec->fpc', frames.astype(jnp.float32), w_qkv.astype(jnp.float32)).astype(jnp.bfloat16)
    split_heads = mixed_qkv.reshape(frame_count, length, 3, HEADS, HDIM)
    scores = jnp.einsum('fqhd,fkhd->fhqk', split_heads[:, :, 0].astype(jnp.float32), split_heads[:, :, 1].astype(jnp.float32)) * HDIM ** (-0.5)
    attn_probs = jax.nn.softmax(scores, axis=-1)
    weights = attn_probs.astype(jnp.bfloat16)
    attended = jnp.einsum('fhqk,fkhd->fqhd', weights.astype(jnp.float32), split_heads[:, :, 2].astype(jnp.float32))
    summed = frames.astype(jnp.float32) + attended.reshape(frame_count, length, vis_width)
    centred = summed - lax.optimization_barrier(jnp.mean(summed, axis=-1, keepdims=True))
    inverse = lax.rsqrt(lax.optimization_barrier(jnp.mean(centred * centred, axis=-1, keepdims=True)) + 1e-06)
    normal_part = centred * inverse
    embedded = (normal_part * ln_gain.astype(jnp.float32)).astype(jnp.bfloat16)
    return (embedded.reshape(frame_count * length // 4, 4 * vis_width), mixed_qkv, attn_probs, normal_part, inverse)

def encoder_backward(w_qkv, ln_gain, mixed_qkv, attn_probs, normal_part, inverse, grad_embed):
    frame_count = normal_part.shape[0]
    length = normal_part.shape[1]
    vis_width = normal_part.shape[2]
    split_heads = mixed_qkv.reshape(frame_count, length, 3, HEADS, HDIM)
    query_heads = split_heads[:, :, 0].astype(jnp.float32)
    key_heads = split_heads[:, :, 1].astype(jnp.float32)
    value_heads = split_heads[:, :, 2].astype(jnp.float32)
    weights = attn_probs.astype(jnp.bfloat16)
    grad_norm = grad_embed.reshape(frame_count, length, vis_width).astype(jnp.float32) * ln_gain.astype(jnp.float32)
    grad_summed = inverse * (grad_norm - lax.optimization_barrier(jnp.mean(grad_norm, axis=-1, keepdims=True)) - normal_part * lax.optimization_barrier(jnp.mean(grad_norm * normal_part, axis=-1, keepdims=True)))
    grad_heads = grad_summed.astype(jnp.bfloat16).reshape(frame_count, length, HEADS, HDIM).astype(jnp.float32)
    grad_weights = jnp.einsum('fqhd,fkhd->fhqk', grad_heads, value_heads)
    grad_values = jnp.einsum('fhqk,fqhd->fkhd', weights.astype(jnp.float32), grad_heads).astype(jnp.bfloat16)
    grad_scores = (attn_probs * (grad_weights - lax.optimization_barrier(jnp.sum(grad_weights * attn_probs, axis=-1, keepdims=True))) * HDIM ** (-0.5)).astype(jnp.bfloat16)
    grad_query = jnp.einsum('fhqk,fkhd->fqhd', grad_scores.astype(jnp.float32), key_heads).astype(jnp.bfloat16)
    grad_keys = jnp.einsum('fhqk,fqhd->fkhd', grad_scores.astype(jnp.float32), query_heads).astype(jnp.bfloat16)
    grad_mixed = jnp.stack([grad_query, grad_keys, grad_values], axis=2).reshape(frame_count, length, 3 * vis_width)
    through = jnp.einsum('fpc,ec->fpe', grad_mixed.astype(jnp.float32), w_qkv.astype(jnp.float32))
    return (grad_summed + through).astype(jnp.bfloat16)

def reference(frames, counts, w_qkv, ln_gain, w_proj, rms_gain, cotangent):
    embedded, mixed_qkv, attn_probs, normal_part, inverse = encoder_forward(frames[0], w_qkv[0], ln_gain[0])
    activations = jnp.dot(embedded, w_proj[1], preferred_element_type=jnp.float32)
    row_count = activations.shape[0]
    position = jnp.arange(row_count, dtype=jnp.int32)
    frame_index = position // TOKF
    live_limit = counts[frame_index // FR_DEV]
    live_mask = (frame_index % FR_DEV < live_limit).astype(jnp.float32)
    inverse_rms = lax.rsqrt(lax.optimization_barrier(jnp.mean(activations * activations, axis=1, keepdims=True)) + 1e-06)
    scaled = rms_gain[1].astype(jnp.float32)[None, :] * cotangent[1].astype(jnp.float32) * live_mask[:, None]
    product = lax.optimization_barrier(jnp.mean(activations * scaled, axis=1, keepdims=True))
    grad_acts = (inverse_rms * scaled - activations * inverse_rms ** 3 * product).astype(jnp.bfloat16)
    block_width = D // N_TP
    proj_used = w_proj[1]

    def add_block(running, block_index):
        block_start = block_index * block_width
        grad_cols = lax.dynamic_slice_in_dim(grad_acts, block_start, block_width, 1)
        proj_cols = lax.dynamic_slice_in_dim(proj_used, block_start, block_width, 1)
        block_term = lax.dot_general(grad_cols, proj_cols, (((1,), (1,)), ((), ())), preferred_element_type=jnp.float32)
        rounded = lax.optimization_barrier(block_term.astype(jnp.bfloat16))
        return (running + rounded.astype(jnp.float32), None)
    running, _ = lax.scan(add_block, jnp.zeros((row_count, DM), jnp.float32), jnp.arange(N_TP, dtype=jnp.int32))
    grad_embed = running.astype(jnp.bfloat16)
    frame_grad = encoder_backward(w_qkv[0], ln_gain[0], mixed_qkv, attn_probs, normal_part, inverse, grad_embed)
    return jnp.stack([frame_grad, jnp.zeros_like(frame_grad)])
```

```python
import jax
import jax.numpy as jnp
from jax import lax
from jax.sharding import PartitionSpec as P

HEADS = 16
HDIM = 80
D = 8192


def passed_along(block, axis, distance):
    devices = range(lax.axis_size(axis))
    route = [(i - distance, i) for i in devices if i - distance in devices]
    return lax.ppermute(block, axis, route)


def encoder_forward(frames, w_qkv, ln_gain):
    frame_count = frames.shape[0]
    length = frames.shape[1]
    vis_width = frames.shape[2]
    mixed_qkv = jnp.einsum("fpe,ec->fpc", frames, w_qkv, preferred_element_type=jnp.float32).astype(
        jnp.bfloat16
    )
    split_heads = mixed_qkv.reshape(frame_count, length, 3, HEADS, HDIM)
    scores = jnp.einsum(
        "fqhd,fkhd->fhqk",
        split_heads[:, :, 0],
        split_heads[:, :, 1],
        preferred_element_type=jnp.float32,
    ) * HDIM ** (-0.5)
    attn_probs = jax.nn.softmax(scores, axis=-1)
    weights = attn_probs.astype(jnp.bfloat16)
    attended = jnp.einsum(
        "fhqk,fkhd->fqhd", weights, split_heads[:, :, 2], preferred_element_type=jnp.float32
    )
    summed = frames.astype(jnp.float32) + attended.reshape(frame_count, length, vis_width)
    centred = summed - jnp.mean(summed, axis=-1, keepdims=True)
    inverse = lax.rsqrt(jnp.mean(centred * centred, axis=-1, keepdims=True) + 1e-06)
    normal_part = centred * inverse
    embedded = (normal_part * ln_gain.astype(jnp.float32)).astype(jnp.bfloat16)
    return (
        embedded.reshape(frame_count * length // 4, 4 * vis_width),
        mixed_qkv,
        attn_probs,
        normal_part,
        inverse,
    )


def encoder_backward(w_qkv, ln_gain, mixed_qkv, attn_probs, normal_part, inverse, grad_embed):
    frame_count = normal_part.shape[0]
    length = normal_part.shape[1]
    vis_width = normal_part.shape[2]
    split_heads = mixed_qkv.reshape(frame_count, length, 3, HEADS, HDIM)
    query_heads = split_heads[:, :, 0]
    key_heads = split_heads[:, :, 1]
    value_heads = split_heads[:, :, 2]
    weights = attn_probs.astype(jnp.bfloat16)
    grad_norm = grad_embed.reshape(frame_count, length, vis_width).astype(
        jnp.float32
    ) * ln_gain.astype(jnp.float32)
    grad_summed = inverse * (
        grad_norm
        - jnp.mean(grad_norm, axis=-1, keepdims=True)
        - normal_part * jnp.mean(grad_norm * normal_part, axis=-1, keepdims=True)
    )
    grad_heads = grad_summed.astype(jnp.bfloat16).reshape(frame_count, length, HEADS, HDIM)
    grad_weights = jnp.einsum(
        "fqhd,fkhd->fhqk", grad_heads, value_heads, preferred_element_type=jnp.float32
    )
    grad_values = jnp.einsum(
        "fhqk,fqhd->fkhd", weights, grad_heads, preferred_element_type=jnp.float32
    ).astype(jnp.bfloat16)
    grad_scores = (
        attn_probs
        * (grad_weights - jnp.sum(grad_weights * attn_probs, axis=-1, keepdims=True))
        * HDIM ** (-0.5)
    ).astype(jnp.bfloat16)
    grad_query = jnp.einsum(
        "fhqk,fkhd->fqhd", grad_scores, key_heads, preferred_element_type=jnp.float32
    ).astype(jnp.bfloat16)
    grad_keys = jnp.einsum(
        "fhqk,fqhd->fkhd", grad_scores, query_heads, preferred_element_type=jnp.float32
    ).astype(jnp.bfloat16)
    grad_mixed = jnp.stack([grad_query, grad_keys, grad_values], axis=2).reshape(
        frame_count, length, 3 * vis_width
    )
    through = jnp.einsum("fpc,ec->fpe", grad_mixed, w_qkv, preferred_element_type=jnp.float32)
    return (grad_summed + through).astype(jnp.bfloat16)


def rotated(blocks, shift):
    count = blocks.shape[0]
    step = 1
    while step < count:
        turned = jnp.concatenate([blocks[step:], blocks[:step]], axis=0)
        blocks = jnp.where((shift // step) % 2 == 1, turned, blocks)
        step *= 2
    return blocks


def flipped(pairs, odd):
    return jnp.where(odd == 1, pairs[:, ::-1], pairs)


def sent_round(block, distance):
    count = lax.axis_size("dp")
    return lax.ppermute(block, "dp", [(i, (i + 2 * distance) % count) for i in range(count)])


def sent_across(block):
    return lax.ppermute(block, "dp", [(i, i ^ 1) for i in range(lax.axis_size("dp"))])


def per_device(frames, counts, w_qkv, ln_gain, w_proj, rms_gain, cotangent):
    f32, bf16 = jnp.float32, jnp.bfloat16
    is_encoder = lax.axis_index("grp") == 0
    dp_count, tp_count = lax.axis_size("dp"), lax.axis_size("tp")
    pair_count = dp_count // 2
    dp_index, tp_index = lax.axis_index("dp"), lax.axis_index("tp")
    pair, odd = dp_index // 2, dp_index % 2

    local_frames = frames[0]
    weight_mix = w_qkv[0]
    gain_ln = ln_gain[0]
    frame_count, length, vis_width = local_frames.shape
    merged_width = 4 * vis_width
    tokens_frame = length // 4
    tokens_here = frame_count * tokens_frame
    rows = tokens_here * tp_count
    depth = w_proj.shape[1]
    half = w_proj.shape[2] // 2
    first = half * 11 // 16 // 128 * 128
    second = half - first

    w_mine = w_proj[0]
    got_first = passed_along(w_mine[:, :first], "grp", -1)
    got_second = passed_along(w_mine[:, first:half], "grp", -1)
    got_cot = passed_along(cotangent[0][:, :half], "grp", -1)
    got_gain = passed_along(rms_gain[:, :half], "grp", -1)
    w_first = jnp.where(is_encoder, got_first, w_mine[:, half : half + first])
    w_second = jnp.where(is_encoder, got_second, w_mine[:, half + first :])
    cot = jnp.where(is_encoder, got_cot, cotangent[0][:, half:])
    gain_rms = jnp.where(is_encoder, got_gain, rms_gain[:, half:])[0]

    def run_encoder():
        return encoder_forward(local_frames, weight_mix, gain_ln)

    def skip_encoder():
        return (
            jnp.zeros((tokens_here, merged_width), bf16),
            jnp.zeros((frame_count, length, 3 * vis_width), bf16),
            jnp.zeros((frame_count, HEADS, length, length), f32),
            jnp.zeros((frame_count, length, vis_width), f32),
            jnp.zeros((frame_count, length, 1), f32),
        )

    embedded, mixed_qkv, attn_probs, normal_part, inverse = lax.cond(
        is_encoder, run_encoder, skip_encoder
    )

    pieces = embedded.reshape(tokens_here, dp_count, depth).transpose(1, 0, 2)
    swapped = lax.all_to_all(pieces, "dp", 0, 0)
    arrived = passed_along(swapped, "grp", 1)
    features = jnp.where(is_encoder, swapped, arrived)
    features = lax.all_gather(features, "tp", axis=1)
    features = features.reshape(pair_count, 2, rows, depth)
    features = flipped(rotated(features, pair), odd)

    def product(block, weight):
        return jnp.einsum("...rk,kc->...rc", block, weight, preferred_element_type=f32)

    away = product(features[:, 1], w_first).astype(bf16)
    away = sent_across(away)
    home = product(features[:, 0], w_first) + away.astype(f32)
    home_sent = home.astype(bf16)
    parts = [sent_round(home_sent[s], s) for s in range(1, pair_count)]
    acts_first = home[0]
    around = [
        sent_round(product(features[s], w_second).astype(bf16), s) for s in range(1, pair_count)
    ]
    both = product(features[0], w_second)
    for block in around:
        both = both + block.astype(f32)
    other = sent_across(both[1].astype(bf16))
    acts_second = both[0] + other.astype(f32)
    for block in parts:
        acts_first = acts_first + block.astype(f32)

    position = lax.broadcasted_iota(jnp.int32, (rows,), 0)
    source = position // tokens_here
    slot_index = position // tokens_frame % frame_count
    owner_hits = source[:, None] == lax.broadcasted_iota(jnp.int32, (1, tp_count), 1)
    live_limit = jnp.sum(jnp.where(owner_hits, counts[None, :], 0), axis=1)
    live_mask = (slot_index < live_limit).astype(f32)
    scaled = gain_rms.astype(f32)[None, :] * cot.astype(f32) * live_mask[:, None]
    scaled_first, scaled_second = scaled[:, :first], scaled[:, first:]
    squares = jnp.sum(acts_first * acts_first, axis=1) + jnp.sum(acts_second * acts_second, axis=1)
    products = jnp.sum(acts_first * scaled_first, axis=1) + jnp.sum(
        acts_second * scaled_second, axis=1
    )
    total_sq, total_prod = lax.psum((squares, products), ("grp", "tp"))
    inverse_rms = lax.rsqrt(total_sq / D + 1e-06)[:, None]
    fall = inverse_rms**3 * (total_prod / D)[:, None]
    grad_first = (inverse_rms * scaled_first - acts_first * fall).astype(bf16)
    grad_second = (inverse_rms * scaled_second - acts_second * fall).astype(bf16)

    row_first = [grad_first] + [None] * (pair_count - 1)
    for s in range(1, pair_count):
        row_first[pair_count - s] = sent_round(grad_first, s)
    row_first = jnp.stack(row_first)
    all_first = jnp.stack([row_first, sent_across(row_first)], axis=1)
    duo = jnp.stack([grad_second, sent_across(grad_second)])
    all_second = [duo] + [None] * (pair_count - 1)
    for s in range(1, pair_count):
        all_second[pair_count - s] = sent_round(duo, s)
    all_second = jnp.stack(all_second)

    def back(block, weight):
        return jnp.einsum("pjrc,kc->pjrk", block, weight, preferred_element_type=f32)

    terms = back(all_first, w_first) + back(all_second, w_second)
    terms = rotated(flipped(terms, odd), (pair_count - pair) % pair_count)
    terms = terms.reshape(dp_count, tp_count, tokens_here, depth).transpose(1, 0, 2, 3)
    terms = rotated(terms, tp_index)
    total = terms[0]
    for s in range(1, tp_count):
        route = [(i, (i + s) % tp_count) for i in range(tp_count)]
        total = total + lax.ppermute(terms[s].astype(bf16), "tp", route).astype(f32)
    returned = passed_along(total.astype(bf16), "grp", -1)
    whole = (total + returned.astype(f32)).astype(bf16)
    whole = lax.all_to_all(whole, "dp", 0, 0)
    grad_embed = whole.transpose(1, 0, 2).reshape(tokens_here, merged_width)

    grad_frames = lax.cond(
        is_encoder,
        lambda: encoder_backward(
            weight_mix, gain_ln, mixed_qkv, attn_probs, normal_part, inverse, grad_embed
        ),
        lambda: jnp.zeros(local_frames.shape, bf16),
    )
    return grad_frames[None]


def solution(mesh):
    placed = (
        P("grp", ("dp", "tp"), None, None),
        P("dp"),
        P("grp", None, None),
        P("grp", None),
        P("grp", "dp", "tp"),
        P("grp", "tp"),
        P("grp", "dp", "tp"),
    )
    return jax.shard_map(
        per_device,
        mesh=mesh,
        in_specs=placed,
        out_specs=P("grp", ("dp", "tp"), None, None),
        check_vma=False,
    )
```

```python
import jax
import jax.numpy as jnp
from jax import lax
from jax.experimental import pallas as pl
from jax.experimental.pallas import tpu as pltpu
from jax.sharding import PartitionSpec as P

HEADS = 16
HDIM = 80
D = 8192
TOKF = 32
CHUNK = 640
CHUNK_HEADS = CHUNK // HDIM


def head_window(head):
    low, high = head * HDIM, (head + 1) * HDIM
    start, stop = low // 128 * 128, -(-high // 128) * 128
    return start, stop, low - start, high - start


def head_only(block, low, high):
    lane = lax.broadcasted_iota(jnp.int32, block.shape, 1)
    return jnp.where((lane >= low) & (lane < high), block, jnp.zeros_like(block))


def dot(a, b, dims):
    return lax.dot_general(a, b, (dims, ((), ())), preferred_element_type=jnp.float32)


NT = ((1,), (1,))
NN = ((1,), (0,))
TN = ((0,), (0,))


def token_order(length):
    row = lax.broadcasted_iota(jnp.int32, (length, length), 0)
    column = lax.broadcasted_iota(jnp.int32, (length, length), 1)
    tokens = length // 4
    return (row % tokens * 4 + row // tokens == column).astype(jnp.bfloat16)


def weight_copies(w_hbm, w_buf, sems):
    return [
        pltpu.make_async_copy(
            w_hbm.at[:, pl.ds(((i % 3) * 2 + i // 3) * CHUNK, CHUNK)], w_buf.at[i], sems.at[i]
        )
        for i in range(6)
    ]


def encoder_forward_kernel(
    x_ref, gain_ref, w_hbm, emb_ref, qkv_ref, probs_ref, norm_ref, inv_ref, w_buf, work, sems
):
    copies = weight_copies(w_hbm, w_buf, sems)
    for copy in copies:
        copy.start()
    x = x_ref[...]
    vis = x.shape[1]
    for half in range(2):
        for kind in range(3):
            i = half * 3 + kind
            copies[i].wait()
            qkv_ref[i] = dot(x, w_buf[i], NN).astype(jnp.bfloat16)
        work[half] = x[:, half * CHUNK : (half + 1) * CHUNK].astype(jnp.float32)
        for head in range(CHUNK_HEADS):
            start, stop, low, high = head_window(head)
            query = qkv_ref[half * 3, :, start:stop]
            key = head_only(qkv_ref[half * 3 + 1, :, start:stop], low, high)
            value = head_only(qkv_ref[half * 3 + 2, :, start:stop], low, high)
            scores = dot(query, key, NT) * HDIM ** (-0.5)
            weights = jnp.exp(scores - jnp.max(scores, axis=1, keepdims=True))
            weights = weights / jnp.sum(weights, axis=1, keepdims=True)
            probs_ref[half * CHUNK_HEADS + head] = weights
            work[half, :, start:stop] += dot(weights.astype(jnp.bfloat16), value, NN)
    first, second = work[0], work[1]
    mean = (
        jnp.sum(first, axis=1, keepdims=True) + jnp.sum(second, axis=1, keepdims=True)
    ) / vis
    first, second = first - mean, second - mean
    variance = (
        jnp.sum(first * first, axis=1, keepdims=True)
        + jnp.sum(second * second, axis=1, keepdims=True)
    ) / vis
    inverse = lax.rsqrt(variance + 1e-06)
    inv_ref[...] = inverse
    gain = gain_ref[...].astype(jnp.float32)
    tokens = x.shape[0] // 4
    order = token_order(x.shape[0])
    for half, centred in enumerate((first, second)):
        normal = centred * inverse
        norm_ref[half] = normal
        embedded = (normal * gain[:, half * CHUNK : (half + 1) * CHUNK]).astype(jnp.bfloat16)
        embedded = dot(order, embedded, NN).astype(jnp.bfloat16)
        for j in range(4):
            emb_ref[j * 2 + half] = embedded[j * tokens : (j + 1) * tokens]


def encoder_forward(frame, w_qkv, ln_gain):
    length, vis = frame.shape
    bf16, f32 = jnp.bfloat16, jnp.float32
    vmem = pl.BlockSpec(memory_space=pltpu.VMEM)
    return pl.pallas_call(
        encoder_forward_kernel,
        out_shape=(
            jax.ShapeDtypeStruct((8, length // 4, CHUNK), bf16),
            jax.ShapeDtypeStruct((6, length, CHUNK), bf16),
            jax.ShapeDtypeStruct((HEADS, length, length), f32),
            jax.ShapeDtypeStruct((2, length, CHUNK), f32),
            jax.ShapeDtypeStruct((length, 1), f32),
        ),
        in_specs=[vmem, vmem, pl.BlockSpec(memory_space=pltpu.HBM)],
        out_specs=(vmem,) * 5,
        scratch_shapes=[
            pltpu.VMEM((6, vis, CHUNK), bf16),
            pltpu.VMEM((2, length, CHUNK), f32),
            pltpu.SemaphoreType.DMA((6,)),
        ],
        compiler_params=pltpu.CompilerParams(vmem_limit_bytes=40 << 20),
        cost_estimate=pl.CostEstimate(flops=1000, transcendentals=0, bytes_accessed=1000),
        name="encoder_forward",
    )(frame, ln_gain, w_qkv)


def encoder_backward_kernel(
    flag_ref,
    grad_ref,
    gain_ref,
    qkv_ref,
    probs_ref,
    norm_ref,
    inv_ref,
    w_hbm,
    out_ref,
    w_buf,
    work,
    mix,
    sems,
):
    f32, bf16 = jnp.float32, jnp.bfloat16
    copies = weight_copies(w_hbm, w_buf, sems)
    for copy in copies:
        copy.start()
    vis = w_hbm.shape[0]
    tokens = grad_ref.shape[1]
    gain = gain_ref[...].astype(f32)
    order = token_order(4 * tokens)
    for half in range(2):
        grads = jnp.concatenate([grad_ref[j * 2 + half] for j in range(4)], axis=0)
        work[half] = dot(order, grads, TN) * gain[:, half * CHUNK : (half + 1) * CHUNK]
    mean = (
        jnp.sum(work[0], axis=1, keepdims=True) + jnp.sum(work[1], axis=1, keepdims=True)
    ) / vis
    along = (
        jnp.sum(work[0] * norm_ref[0], axis=1, keepdims=True)
        + jnp.sum(work[1] * norm_ref[1], axis=1, keepdims=True)
    ) / vis
    inverse = inv_ref[...]
    for half in range(2):
        work[half] = inverse * (work[half] - mean - norm_ref[half] * along)
    total = jnp.zeros((work.shape[1], vis), f32)
    for half in range(2):
        mixed = [jnp.zeros((work.shape[1], CHUNK), f32) for _ in range(3)]
        for kind in range(3):
            mix[kind] = mixed[kind]
        for head in range(CHUNK_HEADS):
            start, stop, low, high = head_window(head)
            grad = head_only(work[half, :, start:stop].astype(bf16), low, high)
            query = head_only(qkv_ref[half * 3, :, start:stop], low, high)
            key = head_only(qkv_ref[half * 3 + 1, :, start:stop], low, high)
            value = qkv_ref[half * 3 + 2, :, start:stop]
            probs = probs_ref[half * CHUNK_HEADS + head]
            grad_weights = dot(grad, value, NT)
            mix[2, :, start:stop] += dot(probs.astype(bf16), grad, TN)
            inner = jnp.sum(grad_weights * probs, axis=1, keepdims=True)
            scores = (probs * (grad_weights - inner) * HDIM ** (-0.5)).astype(bf16)
            mix[0, :, start:stop] += dot(scores, key, NN)
            mix[1, :, start:stop] += dot(scores, query, TN)
        for kind in range(3):
            i = half * 3 + kind
            copies[i].wait()
            total = total + dot(mix[kind].astype(bf16), w_buf[i], NT)
    keep = flag_ref[0] == 1
    for half in range(2):
        columns = slice(half * CHUNK, (half + 1) * CHUNK)
        result = work[half] + total[:, columns]
        out_ref[:, columns] = jnp.where(keep, result, jnp.zeros_like(result)).astype(bf16)


def encoder_backward(flag, w_qkv, ln_gain, qkv, probs, norm, inverse, grad):
    length, vis = norm.shape[1], w_qkv.shape[0]
    bf16, f32 = jnp.bfloat16, jnp.float32
    vmem = pl.BlockSpec(memory_space=pltpu.VMEM)
    return pl.pallas_call(
        encoder_backward_kernel,
        out_shape=jax.ShapeDtypeStruct((length, vis), bf16),
        in_specs=[pl.BlockSpec(memory_space=pltpu.SMEM)]
        + [vmem] * 6
        + [pl.BlockSpec(memory_space=pltpu.HBM)],
        out_specs=vmem,
        scratch_shapes=[
            pltpu.VMEM((6, vis, CHUNK), bf16),
            pltpu.VMEM((2, length, CHUNK), f32),
            pltpu.VMEM((3, length, CHUNK), f32),
            pltpu.SemaphoreType.DMA((6,)),
        ],
        compiler_params=pltpu.CompilerParams(vmem_limit_bytes=40 << 20),
        cost_estimate=pl.CostEstimate(flops=1000, transcendentals=0, bytes_accessed=1000),
        name="encoder_backward",
    )(flag, grad, ln_gain, qkv, probs, norm, inverse, w_qkv)


def split_columns_kernel(bounds, flag_ref, *refs):
    count = len(bounds)
    sources, outs, sems = refs[:-count - 1], refs[-count - 1 : -1], refs[-1]

    @pl.when(flag_ref[0] == 0)
    def _():
        copies = [
            pltpu.make_async_copy(
                sources[which].at[:, pl.ds(start, size)], outs[i], sems.at[i]
            )
            for i, (which, start, size) in enumerate(bounds)
        ]
        for copy in copies:
            copy.start()
        for copy in copies:
            copy.wait()


def split_columns(flag, sources, bounds):
    hbm = pl.BlockSpec(memory_space=pltpu.HBM)
    return pl.pallas_call(
        lambda *refs: split_columns_kernel(bounds, *refs),
        out_shape=tuple(
            jax.ShapeDtypeStruct((sources[which].shape[0], size), sources[which].dtype)
            for which, _, size in bounds
        ),
        in_specs=[pl.BlockSpec(memory_space=pltpu.SMEM)] + [hbm] * len(sources),
        out_specs=(hbm,) * len(bounds),
        scratch_shapes=[pltpu.SemaphoreType.DMA((len(bounds),))],
        name="split_columns",
    )(flag, *sources)


def arrange_in_kernel(flag_ref, order_ref, a_ref, b_ref, out_ref):
    keep = flag_ref[0] == 1
    for r in range(out_ref.shape[0]):
        place = order_ref[r]
        out_ref[r] = jnp.where(keep, a_ref[place], b_ref[place])


def arrange_out_kernel(order_ref, a_ref, b_ref, out_ref):
    for r in range(out_ref.shape[0]):
        value = a_ref[r].astype(jnp.float32) + b_ref[r].astype(jnp.float32)
        out_ref[order_ref[r]] = value.astype(out_ref.dtype)


def arrange(kernel, name, scalars, a, b):
    vmem = pl.BlockSpec(memory_space=pltpu.VMEM)
    return pl.pallas_call(
        kernel,
        out_shape=jax.ShapeDtypeStruct(b.shape, b.dtype),
        in_specs=[pl.BlockSpec(memory_space=pltpu.SMEM)] * len(scalars) + [vmem, vmem],
        out_specs=vmem,
        compiler_params=pltpu.CompilerParams(vmem_limit_bytes=32 << 20),
        name=name,
    )(*scalars, a, b)


def passed_along(block, axis, distance):
    devices = range(lax.axis_size(axis))
    route = [(i - distance, i) for i in devices if i - distance in devices]
    return lax.ppermute(block, axis, route)


def rotated(blocks, shift):
    count = blocks.shape[0]
    step = 1
    while step < count:
        turned = jnp.concatenate([blocks[step:], blocks[:step]], axis=0)
        blocks = jnp.where((shift // step) % 2 == 1, turned, blocks)
        step *= 2
    return blocks


def sent_round(block, distance):
    count = lax.axis_size("dp")
    return lax.ppermute(block, "dp", [(i, (i + 2 * distance) % count) for i in range(count)])


def sent_across(block):
    return lax.ppermute(block, "dp", [(i, i ^ 1) for i in range(lax.axis_size("dp"))])


def sent_tp(block, distance):
    count = lax.axis_size("tp")
    return lax.ppermute(block, "tp", [(i, (i + distance) % count) for i in range(count)])


def per_device(frames, counts, w_qkv, ln_gain, w_proj, rms_gain, cotangent):
    f32, bf16 = jnp.float32, jnp.bfloat16
    is_encoder = lax.axis_index("grp") == 0
    flag = is_encoder.astype(jnp.int32).reshape(1)
    dp_count, tp_count = lax.axis_size("dp"), lax.axis_size("tp")
    pair_count = dp_count // 2
    dp_index, tp_index = lax.axis_index("dp"), lax.axis_index("tp")
    relative = jnp.arange(dp_count, dtype=jnp.int32)
    order = (dp_index // 2 + relative // 2) % pair_count * 2 + (dp_index % 2 ^ relative % 2)

    frame = frames[0, 0]
    tokens_here = frame.shape[0] // 4
    depth = w_proj.shape[1]
    half = w_proj.shape[2] // 2
    first = half * 11 // 16 // 128 * 128
    second = half - first

    w_mine, cot_mine = w_proj[0], cotangent[0]
    give_first, give_second, give_cot = split_columns(
        flag, (w_mine, cot_mine), ((0, 0, first), (0, first, second), (1, 0, half))
    )
    got_first = passed_along(give_first, "grp", -1)
    got_second = passed_along(give_second, "grp", -1)
    got_cot = passed_along(give_cot, "grp", -1)
    got_gain = passed_along(rms_gain[:, :half], "grp", -1)

    embedded, qkv, probs, norm, inverse = encoder_forward(frame, w_qkv[0], ln_gain)

    pieces = embedded
    if depth != CHUNK:
        pieces = embedded.reshape(-1, tokens_here, CHUNK // depth, depth)
        pieces = pieces.transpose(0, 2, 1, 3).reshape(dp_count, tokens_here, depth)
    swapped = lax.all_to_all(pieces, "dp", 0, 0)
    arrived = passed_along(swapped, "grp", 1)
    features = arrange(arrange_in_kernel, "arrange_in", (flag, order), swapped, arrived)
    features = jnp.concatenate(
        [features] + [sent_tp(features, tp_count - s) for s in range(1, tp_count)], axis=1
    ).reshape(pair_count, 2, tp_count * tokens_here, depth)

    w_first = jnp.where(is_encoder, got_first, w_mine[:, half : half + first])
    w_second = jnp.where(is_encoder, got_second, w_mine[:, half + first :])
    cot = jnp.where(is_encoder, got_cot, cot_mine[:, half:])
    gain_rms = jnp.where(is_encoder, got_gain, rms_gain[:, half:])

    def product(block, weight):
        return jnp.einsum("...rk,kc->...rc", block, weight, preferred_element_type=f32)

    away = product(features[:, 1], w_first).astype(bf16)
    away = sent_across(away)
    home = product(features[:, 0], w_first) + away.astype(f32)
    home_sent = home.astype(bf16)
    parts = [sent_round(home_sent[s], s) for s in range(1, pair_count)]
    acts_first = home[0]
    around = [
        sent_round(product(features[s], w_second).astype(bf16), s) for s in range(1, pair_count)
    ]
    both = product(features[0], w_second)
    for block in around:
        both = both + block.astype(f32)
    other = sent_across(both[1].astype(bf16))
    acts_second = both[0] + other.astype(f32)
    for block in parts:
        acts_first = acts_first + block.astype(f32)

    slot = lax.broadcasted_iota(jnp.int32, (1, tokens_here), 1) // TOKF
    live_mask = (slot < rotated(counts, tp_index)[:, None]).astype(f32).reshape(-1, 1)
    cot = rotated(cot.reshape(tp_count, tokens_here, half), tp_index).reshape(-1, half)
    scaled = gain_rms.astype(f32) * cot.astype(f32) * live_mask
    scaled_first, scaled_second = scaled[:, :first], scaled[:, first:]
    squares = jnp.sum(acts_first * acts_first, axis=1) + jnp.sum(acts_second * acts_second, axis=1)
    products = jnp.sum(acts_first * scaled_first, axis=1) + jnp.sum(
        acts_second * scaled_second, axis=1
    )
    sums = jnp.stack([squares, products], axis=1).reshape(tp_count, tokens_here, 2)
    sums = lax.psum(rotated(sums, (tp_count - tp_index) % tp_count), ("grp", "tp"))
    sums = rotated(sums, tp_index).reshape(-1, 2)
    inverse_rms = lax.rsqrt(sums[:, :1] / D + 1e-06)
    fall = inverse_rms**3 * (sums[:, 1:] / D)
    grad_first = (inverse_rms * scaled_first - acts_first * fall).astype(bf16)
    grad_second = (inverse_rms * scaled_second - acts_second * fall).astype(bf16)

    row_first = [grad_first] + [None] * (pair_count - 1)
    for s in range(1, pair_count):
        row_first[pair_count - s] = sent_round(grad_first, s)
    row_first = jnp.stack(row_first)
    duo = jnp.stack([grad_second, sent_across(grad_second)])
    row_first, duo = lax.optimization_barrier((row_first, duo))
    row_first = [row_first, sent_across(row_first)]
    all_second = [duo] + [None] * (pair_count - 1)
    for s in range(1, pair_count):
        all_second[pair_count - s] = sent_round(duo, s)
    all_second = jnp.stack(all_second)

    def back(block, weight):
        return jnp.einsum("prc,kc->prk", block, weight, preferred_element_type=f32)

    terms = [
        back(row_first[j], w_first) + back(all_second[:, j], w_second) for j in range(2)
    ]
    terms = jnp.stack(
        [term.reshape(pair_count, tp_count, tokens_here, depth) for term in terms], axis=1
    ).reshape(dp_count, tp_count, tokens_here, depth)
    total = terms[:, 0]
    for s in range(1, tp_count):
        total = total + sent_tp(terms[:, s].astype(bf16), s).astype(f32)
    total = total.astype(bf16)
    returned = passed_along(total, "grp", -1)
    whole = arrange(arrange_out_kernel, "arrange_out", (order,), total, returned)
    whole = lax.all_to_all(whole, "dp", 0, 0)
    if depth != CHUNK:
        whole = whole.reshape(-1, CHUNK // depth, tokens_here, depth)
        whole = whole.transpose(0, 2, 1, 3).reshape(-1, tokens_here, CHUNK)

    grad_frames = encoder_backward(flag, w_qkv[0], ln_gain, qkv, probs, norm, inverse, whole)
    return grad_frames[None, None]


def solution(mesh):
    placed = (
        P("grp", ("dp", "tp"), None, None),
        P("dp"),
        P("grp", None, None),
        P("grp", None),
        P("grp", "dp", "tp"),
        P("grp", "tp"),
        P("grp", "dp", "tp"),
    )
    return jax.shard_map(
        per_device,
        mesh=mesh,
        in_specs=placed,
        out_specs=P("grp", ("dp", "tp"), None, None),
        check_vma=False,
    )
```

```python
import jax
import jax.numpy as jnp
from jax import lax
from jax.experimental import pallas as pl
from jax.experimental.pallas import tpu as pltpu
from jax.sharding import PartitionSpec as P

HEADS = 16
HDIM = 80
D = 8192
TOKF = 32
FIRST_PART = 9
GAIN_ROWS = 16
CHUNK = 640
CHUNK_HEADS = CHUNK // HDIM


def head_window(head):
    low, high = head * HDIM, (head + 1) * HDIM
    start, stop = low // 128 * 128, -(-high // 128) * 128
    return start, stop, low - start, high - start


def head_only(block, low, high):
    lane = lax.broadcasted_iota(jnp.int32, block.shape, 1)
    return jnp.where((lane >= low) & (lane < high), block, jnp.zeros_like(block))


def dot(a, b, dims):
    return lax.dot_general(a, b, (dims, ((), ())), preferred_element_type=jnp.float32)


NT = ((1,), (1,))
NN = ((1,), (0,))
TN = ((0,), (0,))


def token_order(length):
    row = lax.broadcasted_iota(jnp.int32, (length, length), 0)
    column = lax.broadcasted_iota(jnp.int32, (length, length), 1)
    tokens = length // 4
    return (row % tokens * 4 + row // tokens == column).astype(jnp.bfloat16)


def weight_copies(w_hbm, w_buf, sems):
    return [
        pltpu.make_async_copy(
            w_hbm.at[:, pl.ds(((i % 3) * 2 + i // 3) * CHUNK, CHUNK)], w_buf.at[i], sems.at[i]
        )
        for i in range(6)
    ]


def encoder_forward_kernel(
    flag_ref,
    x_ref,
    gain_ref,
    w_hbm,
    emb_ref,
    qkv_hbm,
    probs_hbm,
    norm_hbm,
    inv_ref,
    w_buf,
    qkv_ref,
    probs_ref,
    norm_ref,
    work,
    sems,
    out_sems,
):
    @pl.when(flag_ref[0] == 1)
    def _():
        copies = weight_copies(w_hbm, w_buf, sems)
        for copy in copies:
            copy.start()
        outs = []
        x = x_ref[...]
        vis = x.shape[1]
        for half in range(2):
            for kind in range(3):
                i = half * 3 + kind
                copies[i].wait()
                qkv_ref[i] = dot(x, w_buf[i], NN).astype(jnp.bfloat16)
            heads = pl.ds(half * CHUNK_HEADS, CHUNK_HEADS)
            outs.append(
                pltpu.make_async_copy(
                    qkv_ref.at[pl.ds(half * 3, 3)],
                    qkv_hbm.at[pl.ds(half * 3, 3)],
                    out_sems.at[half],
                )
            )
            outs[-1].start()
            work[half] = x[:, half * CHUNK : (half + 1) * CHUNK].astype(jnp.float32)
            for head in range(CHUNK_HEADS):
                start, stop, low, high = head_window(head)
                query = qkv_ref[half * 3, :, start:stop]
                key = head_only(qkv_ref[half * 3 + 1, :, start:stop], low, high)
                value = head_only(qkv_ref[half * 3 + 2, :, start:stop], low, high)
                scores = dot(query, key, NT) * HDIM ** (-0.5)
                weights = jnp.exp(scores - jnp.max(scores, axis=1, keepdims=True))
                weights = weights / jnp.sum(weights, axis=1, keepdims=True)
                probs_ref[half * CHUNK_HEADS + head] = weights
                work[half, :, start:stop] += dot(weights.astype(jnp.bfloat16), value, NN)
            outs.append(
                pltpu.make_async_copy(probs_ref.at[heads], probs_hbm.at[heads], out_sems.at[2 + half])
            )
            outs[-1].start()
        first, second = work[0], work[1]
        mean = (
            jnp.sum(first, axis=1, keepdims=True) + jnp.sum(second, axis=1, keepdims=True)
        ) / vis
        first, second = first - mean, second - mean
        variance = (
            jnp.sum(first * first, axis=1, keepdims=True)
            + jnp.sum(second * second, axis=1, keepdims=True)
        ) / vis
        inverse = lax.rsqrt(variance + 1e-06)
        inv_ref[...] = inverse
        gain = gain_ref[...].astype(jnp.float32)
        tokens = x.shape[0] // 4
        order = token_order(x.shape[0])
        for half, centred in enumerate((first, second)):
            normal = centred * inverse
            norm_ref[half] = normal
            embedded = (normal * gain[:, half * CHUNK : (half + 1) * CHUNK]).astype(jnp.bfloat16)
            embedded = dot(order, embedded, NN).astype(jnp.bfloat16)
            for j in range(4):
                emb_ref[j * 2 + half] = embedded[j * tokens : (j + 1) * tokens]
        outs.append(pltpu.make_async_copy(norm_ref, norm_hbm, out_sems.at[4]))
        outs[-1].start()
        for copy in outs:
            copy.wait()


def encoder_forward(flag, frame, w_qkv, ln_gain):
    length, vis = frame.shape
    bf16, f32 = jnp.bfloat16, jnp.float32
    vmem = pl.BlockSpec(memory_space=pltpu.VMEM)
    hbm = pl.BlockSpec(memory_space=pltpu.HBM)
    return pl.pallas_call(
        encoder_forward_kernel,
        out_shape=(
            jax.ShapeDtypeStruct((8, length // 4, CHUNK), bf16),
            jax.ShapeDtypeStruct((6, length, CHUNK), bf16),
            jax.ShapeDtypeStruct((HEADS, length, length), f32),
            jax.ShapeDtypeStruct((2, length, CHUNK), f32),
            jax.ShapeDtypeStruct((length, 1), f32),
        ),
        in_specs=[pl.BlockSpec(memory_space=pltpu.SMEM), vmem, vmem, hbm],
        out_specs=(vmem, hbm, hbm, hbm, vmem),
        scratch_shapes=[
            pltpu.VMEM((6, vis, CHUNK), bf16),
            pltpu.VMEM((6, length, CHUNK), bf16),
            pltpu.VMEM((HEADS, length, length), f32),
            pltpu.VMEM((2, length, CHUNK), f32),
            pltpu.VMEM((2, length, CHUNK), f32),
            pltpu.SemaphoreType.DMA((6,)),
            pltpu.SemaphoreType.DMA((5,)),
        ],
        compiler_params=pltpu.CompilerParams(vmem_limit_bytes=40 << 20),
        cost_estimate=pl.CostEstimate(flops=1000, transcendentals=0, bytes_accessed=1000),
        name="encoder_forward",
    )(flag, frame, ln_gain, in_hbm(w_qkv))


def encoder_backward_kernel(
    flag_ref,
    grad_ref,
    gain_ref,
    qkv_ref,
    probs_ref,
    norm_ref,
    inv_ref,
    w_hbm,
    out_ref,
    w_buf,
    work,
    mix,
    sems,
):
    @pl.when(flag_ref[0] == 0)
    def _():
        out_ref[...] = jnp.zeros_like(out_ref)

    @pl.when(flag_ref[0] == 1)
    def _():
        f32, bf16 = jnp.float32, jnp.bfloat16
        copies = weight_copies(w_hbm, w_buf, sems)
        for copy in copies:
            copy.start()
        vis = w_hbm.shape[0]
        tokens = grad_ref.shape[1]
        gain = gain_ref[...].astype(f32)
        order = token_order(4 * tokens)
        for half in range(2):
            grads = jnp.concatenate([grad_ref[j * 2 + half] for j in range(4)], axis=0)
            work[half] = dot(order, grads, TN) * gain[:, half * CHUNK : (half + 1) * CHUNK]
        mean = (
            jnp.sum(work[0], axis=1, keepdims=True) + jnp.sum(work[1], axis=1, keepdims=True)
        ) / vis
        along = (
            jnp.sum(work[0] * norm_ref[0], axis=1, keepdims=True)
            + jnp.sum(work[1] * norm_ref[1], axis=1, keepdims=True)
        ) / vis
        inverse = inv_ref[...]
        for half in range(2):
            work[half] = inverse * (work[half] - mean - norm_ref[half] * along)
        total = jnp.zeros((work.shape[1], vis), f32)
        for half in range(2):
            mixed = [jnp.zeros((work.shape[1], CHUNK), f32) for _ in range(3)]
            for kind in range(3):
                mix[kind] = mixed[kind]
            for head in range(CHUNK_HEADS):
                start, stop, low, high = head_window(head)
                grad = head_only(work[half, :, start:stop].astype(bf16), low, high)
                query = head_only(qkv_ref[half * 3, :, start:stop], low, high)
                key = head_only(qkv_ref[half * 3 + 1, :, start:stop], low, high)
                value = qkv_ref[half * 3 + 2, :, start:stop]
                probs = probs_ref[half * CHUNK_HEADS + head]
                grad_weights = dot(grad, value, NT)
                mix[2, :, start:stop] += dot(probs.astype(bf16), grad, TN)
                inner = jnp.sum(grad_weights * probs, axis=1, keepdims=True)
                scores = (probs * (grad_weights - inner) * HDIM ** (-0.5)).astype(bf16)
                mix[0, :, start:stop] += dot(scores, key, NN)
                mix[1, :, start:stop] += dot(scores, query, TN)
            for kind in range(3):
                i = half * 3 + kind
                copies[i].wait()
                total = total + dot(mix[kind].astype(bf16), w_buf[i], NT)
        for half in range(2):
            columns = slice(half * CHUNK, (half + 1) * CHUNK)
            out_ref[:, columns] = (work[half] + total[:, columns]).astype(bf16)


def encoder_backward(flag, w_qkv, ln_gain, qkv, probs, norm, inverse, grad):
    length, vis = norm.shape[1], w_qkv.shape[0]
    bf16, f32 = jnp.bfloat16, jnp.float32
    vmem = pl.BlockSpec(memory_space=pltpu.VMEM)
    return pl.pallas_call(
        encoder_backward_kernel,
        out_shape=jax.ShapeDtypeStruct((length, vis), bf16),
        in_specs=[pl.BlockSpec(memory_space=pltpu.SMEM)]
        + [vmem] * 6
        + [pl.BlockSpec(memory_space=pltpu.HBM)],
        out_specs=vmem,
        scratch_shapes=[
            pltpu.VMEM((6, vis, CHUNK), bf16),
            pltpu.VMEM((2, length, CHUNK), f32),
            pltpu.VMEM((3, length, CHUNK), f32),
            pltpu.SemaphoreType.DMA((6,)),
        ],
        compiler_params=pltpu.CompilerParams(vmem_limit_bytes=40 << 20),
        cost_estimate=pl.CostEstimate(flops=1000, transcendentals=0, bytes_accessed=1000),
        name="encoder_backward",
    )(flag, grad, ln_gain, qkv, probs, norm, inverse, in_hbm(w_qkv))


def give_columns_kernel(start, flag_ref, after_ref, w_hbm, out_ref, sem):
    @pl.when(flag_ref[0] == 0)
    def _():
        copy = pltpu.make_async_copy(w_hbm.at[:, pl.ds(start, out_ref.shape[1])], out_ref, sem)
        copy.start()
        copy.wait()


def give_columns(flag, after, matrix, start, size):
    return pl.pallas_call(
        lambda *refs: give_columns_kernel(start, *refs),
        out_shape=jax.ShapeDtypeStruct((matrix.shape[0], size), matrix.dtype),
        in_specs=[
            pl.BlockSpec(memory_space=pltpu.SMEM),
            pl.BlockSpec(memory_space=pl.ANY),
            pl.BlockSpec(memory_space=pltpu.HBM),
        ],
        out_specs=pl.BlockSpec(memory_space=pltpu.VMEM),
        scratch_shapes=[pltpu.SemaphoreType.DMA],
        compiler_params=pltpu.CompilerParams(vmem_limit_bytes=16 << 20),
        cost_estimate=pl.CostEstimate(flops=1000, transcendentals=0, bytes_accessed=1000),
        name="give_columns",
    )(flag, after, in_hbm(matrix))


def give_cotangent_kernel(flag_ref, after_ref, gain_ref, cot_hbm, out_ref, sem):
    @pl.when(flag_ref[0] == 0)
    def _():
        rows, size = cot_hbm.shape[0], out_ref.shape[1]
        copy = pltpu.make_async_copy(
            cot_hbm.at[:, pl.ds(0, size)], out_ref.at[pl.ds(0, rows)], sem
        )
        copy.start()
        out_ref[rows:] = jnp.broadcast_to(gain_ref[:, :size], (GAIN_ROWS, size))
        copy.wait()


def give_cotangent(flag, after, gain, cot, size):
    return pl.pallas_call(
        give_cotangent_kernel,
        out_shape=jax.ShapeDtypeStruct((cot.shape[0] + GAIN_ROWS, size), cot.dtype),
        in_specs=[
            pl.BlockSpec(memory_space=pltpu.SMEM),
            pl.BlockSpec(memory_space=pl.ANY),
            pl.BlockSpec(memory_space=pltpu.VMEM),
            pl.BlockSpec(memory_space=pltpu.HBM),
        ],
        out_specs=pl.BlockSpec(memory_space=pltpu.VMEM),
        scratch_shapes=[pltpu.SemaphoreType.DMA],
        compiler_params=pltpu.CompilerParams(vmem_limit_bytes=16 << 20),
        cost_estimate=pl.CostEstimate(flops=1000, transcendentals=0, bytes_accessed=1000),
        name="give_cotangent",
    )(flag, after, gain, in_hbm(cot))


def in_hbm(array):
    return pltpu.with_memory_space_constraint(array, pltpu.HBM)


def partial_kernel(start, flag_ref, x_ref, got_ref, mine_ref, away_ref, home_ref, w_ref, sem):
    size = w_ref.shape[1]

    @pl.when(flag_ref[0] == 1)
    def _():
        copy = pltpu.make_async_copy(got_ref, w_ref, sem)
        copy.start()
        copy.wait()

    @pl.when(flag_ref[0] == 0)
    def _():
        copy = pltpu.make_async_copy(mine_ref.at[:, pl.ds(start, size)], w_ref, sem)
        copy.start()
        copy.wait()

    pairs, _, rows, depth = x_ref.shape
    weight = w_ref[...]
    away = dot(x_ref[:, 1].reshape(pairs * rows, depth), weight, NN)
    away_ref[...] = away.reshape(away_ref.shape).astype(away_ref.dtype)
    home = dot(x_ref[:, 0].reshape(pairs * rows, depth), weight, NN)
    home_ref[...] = home.reshape(home_ref.shape)


def partial_products(flag, features, got, matrix, start):
    pairs, _, rows, depth = features.shape
    size = got.shape[1]
    vmem = pl.BlockSpec(memory_space=pltpu.VMEM)
    return pl.pallas_call(
        lambda *refs: partial_kernel(start, *refs),
        out_shape=(
            jax.ShapeDtypeStruct((pairs, rows, size), jnp.bfloat16),
            jax.ShapeDtypeStruct((pairs, rows, size), jnp.float32),
            jax.ShapeDtypeStruct((depth, size), got.dtype),
        ),
        in_specs=[
            pl.BlockSpec(memory_space=pltpu.SMEM),
            vmem,
            pl.BlockSpec(memory_space=pl.ANY),
            pl.BlockSpec(memory_space=pltpu.HBM),
        ],
        out_specs=(vmem,) * 3,
        scratch_shapes=[pltpu.SemaphoreType.DMA],
        compiler_params=pltpu.CompilerParams(vmem_limit_bytes=32 << 20),
        cost_estimate=pl.CostEstimate(
            flops=4 * pairs * rows * depth * size, transcendentals=0, bytes_accessed=4 * depth * size
        ),
        name="partial_products",
    )(flag, features, got, in_hbm(matrix))


def arrange_in_kernel(flag_ref, order_ref, a_ref, b_ref, out_ref):
    keep = flag_ref[0] == 1
    for r in range(out_ref.shape[0]):
        place = order_ref[r]
        out_ref[r] = jnp.where(keep, a_ref[place], b_ref[place])


def arrange_out_kernel(order_ref, a_ref, b_ref, out_ref):
    for r in range(out_ref.shape[0]):
        value = a_ref[r].astype(jnp.float32) + b_ref[r].astype(jnp.float32)
        out_ref[order_ref[r]] = value.astype(out_ref.dtype)


def arrange(kernel, name, scalars, a, b):
    vmem = pl.BlockSpec(memory_space=pltpu.VMEM)
    return pl.pallas_call(
        kernel,
        out_shape=jax.ShapeDtypeStruct(b.shape, b.dtype),
        in_specs=[pl.BlockSpec(memory_space=pltpu.SMEM)] * len(scalars) + [vmem, vmem],
        out_specs=vmem,
        compiler_params=pltpu.CompilerParams(vmem_limit_bytes=32 << 20),
        name=name,
    )(*scalars, a, b)


def passed_along(block, axis, distance):
    devices = range(lax.axis_size(axis))
    route = [(i - distance, i) for i in devices if i - distance in devices]
    return lax.ppermute(block, axis, route)


def rotated(blocks, shift):
    count = blocks.shape[0]
    step = 1
    while step < count:
        turned = jnp.concatenate([blocks[step:], blocks[:step]], axis=0)
        blocks = jnp.where((shift // step) % 2 == 1, turned, blocks)
        step *= 2
    return blocks


def sent_round(block, distance):
    count = lax.axis_size("dp")
    return lax.ppermute(block, "dp", [(i, (i + 2 * distance) % count) for i in range(count)])


def sent_across(block):
    return lax.ppermute(block, "dp", [(i, i ^ 1) for i in range(lax.axis_size("dp"))])


def sent_tp(block, distance):
    count = lax.axis_size("tp")
    return lax.ppermute(block, "tp", [(i, (i + distance) % count) for i in range(count)])


def per_device(frames, counts, w_qkv, ln_gain, w_proj, rms_gain, cotangent):
    f32, bf16 = jnp.float32, jnp.bfloat16
    is_encoder = lax.axis_index("grp") == 0
    flag = is_encoder.astype(jnp.int32).reshape(1)
    dp_count, tp_count = lax.axis_size("dp"), lax.axis_size("tp")
    pair_count = dp_count // 2
    dp_index, tp_index = lax.axis_index("dp"), lax.axis_index("tp")
    relative = jnp.arange(dp_count, dtype=jnp.int32)
    order = (dp_index // 2 + relative // 2) % pair_count * 2 + (dp_index % 2 ^ relative % 2)

    frame = frames[0, 0]
    tokens_here = frame.shape[0] // 4
    depth = w_proj.shape[1]
    half = w_proj.shape[2] // 2
    first = half * FIRST_PART // 16 // 128 * 128
    sizes = (first, half - first)

    w_mine, cot_mine = w_proj[0], cotangent[0]
    give = [give_columns(flag, flag, w_mine, 0, sizes[0])]
    give.append(give_columns(flag, give[0], w_mine, first, sizes[1]))
    got = [passed_along(block, "grp", -1) for block in give]
    got_cot = passed_along(give_cotangent(flag, give[1], rms_gain, cot_mine, half), "grp", -1)

    embedded, qkv, probs, norm, inverse = encoder_forward(flag, frame, w_qkv[0], ln_gain)

    pieces = embedded
    if depth != CHUNK:
        pieces = embedded.reshape(-1, tokens_here, CHUNK // depth, depth)
        pieces = pieces.transpose(0, 2, 1, 3).reshape(dp_count, tokens_here, depth)
    swapped = lax.all_to_all(pieces, "dp", 0, 0)
    arrived = passed_along(swapped, "grp", 1)
    features = arrange(arrange_in_kernel, "arrange_in", (flag, order), swapped, arrived)
    features = jnp.concatenate(
        [features] + [sent_tp(features, tp_count - s) for s in range(1, tp_count)], axis=1
    ).reshape(pair_count, 2, tp_count * tokens_here, depth)

    acts, weights = [], []
    for c in range(2):
        away, home, weight = partial_products(flag, features, got[c], w_mine, half + c * first)
        weights.append(weight)
        home = home + sent_across(away).astype(f32)
        sent = home.astype(bf16)
        sent, features = lax.optimization_barrier((sent, features))
        parts = [sent_round(sent[s], s) for s in range(1, pair_count)]
        total = home[0]
        for block in parts:
            total = total + block.astype(f32)
        acts.append(total)

    got_cot, acts[0] = lax.optimization_barrier((got_cot, acts[0]))
    rows = cot_mine.shape[0]
    cot = jnp.where(is_encoder, got_cot[:rows], cot_mine[:, half:])
    gain_rms = jnp.where(is_encoder, got_cot[rows : rows + 1], rms_gain[:, half:])
    slot = lax.broadcasted_iota(jnp.int32, (1, tokens_here), 1) // TOKF
    live_mask = (slot < rotated(counts, tp_index)[:, None]).astype(f32).reshape(-1, 1)
    cot = rotated(cot.reshape(tp_count, tokens_here, half), tp_index).reshape(-1, half)
    scaled = gain_rms.astype(f32) * cot.astype(f32) * live_mask
    scaled = (scaled[:, :first], scaled[:, first:])
    squares = sum(jnp.sum(act * act, axis=1) for act in acts)
    products = sum(jnp.sum(act * part, axis=1) for act, part in zip(acts, scaled))
    sums = jnp.stack([squares, products], axis=1).reshape(tp_count, tokens_here, 2)
    sums = lax.psum(rotated(sums, (tp_count - tp_index) % tp_count), ("grp", "tp"))
    sums = rotated(sums, tp_index).reshape(-1, 2)
    inverse_rms = lax.rsqrt(sums[:, :1] / D + 1e-06)
    fall = inverse_rms**3 * (sums[:, 1:] / D)
    grads = [
        (inverse_rms * part - act * fall).astype(bf16) for act, part in zip(acts, scaled)
    ]

    def gathered_round(block):
        blocks = [block] + [None] * (pair_count - 1)
        for s in range(1, pair_count):
            blocks[pair_count - s] = sent_round(block, s)
        return jnp.stack(blocks)

    near = gathered_round(grads[0])
    duo = jnp.stack([grads[1], sent_across(grads[1])])
    near, duo = lax.optimization_barrier((near, duo))
    far = sent_across(near)
    duos = gathered_round(duo)
    near, far = (near, duos[:, 0]), (far, duos[:, 1])

    def back(blocks):
        return sum(
            jnp.einsum("prc,kc->prk", block, weight, preferred_element_type=f32)
            for block, weight in zip(blocks, weights)
        )

    terms = [back(near), back(far)]
    terms = jnp.stack(
        [term.reshape(pair_count, tp_count, tokens_here, depth) for term in terms], axis=1
    ).reshape(dp_count, tp_count, tokens_here, depth)
    total = terms[:, 0]
    for s in range(1, tp_count):
        total = total + sent_tp(terms[:, s].astype(bf16), s).astype(f32)
    total = total.astype(bf16)
    returned = passed_along(total, "grp", -1)
    whole = arrange(arrange_out_kernel, "arrange_out", (order,), total, returned)
    whole = lax.all_to_all(whole, "dp", 0, 0)
    if depth != CHUNK:
        whole = whole.reshape(-1, CHUNK // depth, tokens_here, depth)
        whole = whole.transpose(0, 2, 1, 3).reshape(-1, tokens_here, CHUNK)

    grad_frames = encoder_backward(flag, w_qkv[0], ln_gain, qkv, probs, norm, inverse, whole)
    return grad_frames[None, None]


def solution(mesh):
    placed = (
        P("grp", ("dp", "tp"), None, None),
        P("dp"),
        P("grp", None, None),
        P("grp", None),
        P("grp", "dp", "tp"),
        P("grp", "tp"),
        P("grp", "dp", "tp"),
    )
    return jax.shard_map(
        per_device,
        mesh=mesh,
        in_specs=placed,
        out_specs=P("grp", ("dp", "tp"), None, None),
        check_vma=False,
    )
```

```python
import jax
import jax.numpy as jnp
from jax import lax
from jax.experimental import pallas as pl
from jax.experimental.pallas import tpu as pltpu
from jax.sharding import PartitionSpec as P

HEADS = 16
HDIM = 80
D = 8192
TOKF = 32
FIRST_PART = 9
GAIN_ROWS = 16
CHUNK = 640
CHUNK_HEADS = CHUNK // HDIM


def head_window(head):
    low, high = head * HDIM, (head + 1) * HDIM
    start, stop = low // 128 * 128, -(-high // 128) * 128
    return start, stop, low - start, high - start


def head_only(block, low, high):
    lane = lax.broadcasted_iota(jnp.int32, block.shape, 1)
    return jnp.where((lane >= low) & (lane < high), block, jnp.zeros_like(block))


def dot(a, b, dims):
    return lax.dot_general(a, b, (dims, ((), ())), preferred_element_type=jnp.float32)


NT = ((1,), (1,))
NN = ((1,), (0,))
TN = ((0,), (0,))


def token_order(length):
    row = lax.broadcasted_iota(jnp.int32, (length, length), 0)
    column = lax.broadcasted_iota(jnp.int32, (length, length), 1)
    tokens = length // 4
    return (row % tokens * 4 + row // tokens == column).astype(jnp.bfloat16)


def weight_copies(w_hbm, w_buf, sems):
    return [
        pltpu.make_async_copy(
            w_hbm.at[:, pl.ds(((i % 3) * 2 + i // 3) * CHUNK, CHUNK)], w_buf.at[i], sems.at[i]
        )
        for i in range(6)
    ]


def encoder_forward_kernel(
    flag_ref,
    x_ref,
    gain_ref,
    w_hbm,
    emb_ref,
    qkv_hbm,
    probs_hbm,
    norm_hbm,
    inv_ref,
    w_buf,
    qkv_ref,
    probs_ref,
    norm_ref,
    work,
    sems,
    out_sems,
):
    @pl.when(flag_ref[0] == 1)
    def _():
        copies = weight_copies(w_hbm, w_buf, sems)
        for copy in copies:
            copy.start()
        outs = []
        x = x_ref[...]
        vis = x.shape[1]
        for half in range(2):
            for kind in range(3):
                i = half * 3 + kind
                copies[i].wait()
                qkv_ref[i] = dot(x, w_buf[i], NN).astype(jnp.bfloat16)
            heads = pl.ds(half * CHUNK_HEADS, CHUNK_HEADS)
            outs.append(
                pltpu.make_async_copy(
                    qkv_ref.at[pl.ds(half * 3, 3)],
                    qkv_hbm.at[pl.ds(half * 3, 3)],
                    out_sems.at[half],
                )
            )
            outs[-1].start()
            work[half] = x[:, half * CHUNK : (half + 1) * CHUNK].astype(jnp.float32)
            for head in range(CHUNK_HEADS):
                start, stop, low, high = head_window(head)
                query = qkv_ref[half * 3, :, start:stop]
                key = head_only(qkv_ref[half * 3 + 1, :, start:stop], low, high)
                value = head_only(qkv_ref[half * 3 + 2, :, start:stop], low, high)
                scores = dot(query, key, NT) * HDIM ** (-0.5)
                weights = jnp.exp(scores - jnp.max(scores, axis=1, keepdims=True))
                weights = weights / jnp.sum(weights, axis=1, keepdims=True)
                probs_ref[half * CHUNK_HEADS + head] = weights
                work[half, :, start:stop] += dot(weights.astype(jnp.bfloat16), value, NN)
            outs.append(
                pltpu.make_async_copy(probs_ref.at[heads], probs_hbm.at[heads], out_sems.at[2 + half])
            )
            outs[-1].start()
        first, second = work[0], work[1]
        mean = (
            jnp.sum(first, axis=1, keepdims=True) + jnp.sum(second, axis=1, keepdims=True)
        ) / vis
        first, second = first - mean, second - mean
        variance = (
            jnp.sum(first * first, axis=1, keepdims=True)
            + jnp.sum(second * second, axis=1, keepdims=True)
        ) / vis
        inverse = lax.rsqrt(variance + 1e-06)
        inv_ref[...] = inverse
        gain = gain_ref[...].astype(jnp.float32)
        tokens = x.shape[0] // 4
        order = token_order(x.shape[0])
        for half, centred in enumerate((first, second)):
            normal = centred * inverse
            norm_ref[half] = normal
            embedded = (normal * gain[:, half * CHUNK : (half + 1) * CHUNK]).astype(jnp.bfloat16)
            embedded = dot(order, embedded, NN).astype(jnp.bfloat16)
            for j in range(4):
                emb_ref[j * 2 + half] = embedded[j * tokens : (j + 1) * tokens]
        outs.append(pltpu.make_async_copy(norm_ref, norm_hbm, out_sems.at[4]))
        outs[-1].start()
        for copy in outs:
            copy.wait()


def encoder_forward(flag, frame, w_qkv, ln_gain):
    length, vis = frame.shape
    bf16, f32 = jnp.bfloat16, jnp.float32
    vmem = pl.BlockSpec(memory_space=pltpu.VMEM)
    hbm = pl.BlockSpec(memory_space=pltpu.HBM)
    return pl.pallas_call(
        encoder_forward_kernel,
        out_shape=(
            jax.ShapeDtypeStruct((8, length // 4, CHUNK), bf16),
            pltpu.HBM((6, length, CHUNK), bf16),
            pltpu.HBM((HEADS, length, length), f32),
            pltpu.HBM((2, length, CHUNK), f32),
            jax.ShapeDtypeStruct((length, 1), f32),
        ),
        in_specs=[pl.BlockSpec(memory_space=pltpu.SMEM), vmem, vmem, hbm],
        out_specs=(vmem, hbm, hbm, hbm, vmem),
        scratch_shapes=[
            pltpu.VMEM((6, vis, CHUNK), bf16),
            pltpu.VMEM((6, length, CHUNK), bf16),
            pltpu.VMEM((HEADS, length, length), f32),
            pltpu.VMEM((2, length, CHUNK), f32),
            pltpu.VMEM((2, length, CHUNK), f32),
            pltpu.SemaphoreType.DMA((6,)),
            pltpu.SemaphoreType.DMA((5,)),
        ],
        compiler_params=pltpu.CompilerParams(vmem_limit_bytes=40 << 20),
        cost_estimate=pl.CostEstimate(flops=1000, transcendentals=0, bytes_accessed=1000),
        name="encoder_forward",
    )(flag, frame, ln_gain, in_hbm(w_qkv))


def encoder_backward_kernel(
    flag_ref,
    grad_ref,
    gain_ref,
    qkv_ref,
    probs_ref,
    norm_ref,
    inv_ref,
    w_hbm,
    out_ref,
    w_buf,
    work,
    mix,
    sems,
):
    @pl.when(flag_ref[0] == 0)
    def _():
        out_ref[...] = jnp.zeros_like(out_ref)

    @pl.when(flag_ref[0] == 1)
    def _():
        f32, bf16 = jnp.float32, jnp.bfloat16
        copies = weight_copies(w_hbm, w_buf, sems)
        for copy in copies:
            copy.start()
        vis = w_hbm.shape[0]
        tokens = grad_ref.shape[1]
        gain = gain_ref[...].astype(f32)
        order = token_order(4 * tokens)
        for half in range(2):
            grads = jnp.concatenate([grad_ref[j * 2 + half] for j in range(4)], axis=0)
            work[half] = dot(order, grads, TN) * gain[:, half * CHUNK : (half + 1) * CHUNK]
        mean = (
            jnp.sum(work[0], axis=1, keepdims=True) + jnp.sum(work[1], axis=1, keepdims=True)
        ) / vis
        along = (
            jnp.sum(work[0] * norm_ref[0], axis=1, keepdims=True)
            + jnp.sum(work[1] * norm_ref[1], axis=1, keepdims=True)
        ) / vis
        inverse = inv_ref[...]
        for half in range(2):
            work[half] = inverse * (work[half] - mean - norm_ref[half] * along)
        total = jnp.zeros((work.shape[1], vis), f32)
        for half in range(2):
            mixed = [jnp.zeros((work.shape[1], CHUNK), f32) for _ in range(3)]
            for kind in range(3):
                mix[kind] = mixed[kind]
            for head in range(CHUNK_HEADS):
                start, stop, low, high = head_window(head)
                grad = head_only(work[half, :, start:stop].astype(bf16), low, high)
                query = head_only(qkv_ref[half * 3, :, start:stop], low, high)
                key = head_only(qkv_ref[half * 3 + 1, :, start:stop], low, high)
                value = qkv_ref[half * 3 + 2, :, start:stop]
                probs = probs_ref[half * CHUNK_HEADS + head]
                grad_weights = dot(grad, value, NT)
                mix[2, :, start:stop] += dot(probs.astype(bf16), grad, TN)
                inner = jnp.sum(grad_weights * probs, axis=1, keepdims=True)
                scores = (probs * (grad_weights - inner) * HDIM ** (-0.5)).astype(bf16)
                mix[0, :, start:stop] += dot(scores, key, NN)
                mix[1, :, start:stop] += dot(scores, query, TN)
            for kind in range(3):
                i = half * 3 + kind
                copies[i].wait()
                total = total + dot(mix[kind].astype(bf16), w_buf[i], NT)
        for half in range(2):
            columns = slice(half * CHUNK, (half + 1) * CHUNK)
            out_ref[:, columns] = (work[half] + total[:, columns]).astype(bf16)


def encoder_backward(flag, w_qkv, ln_gain, qkv, probs, norm, inverse, grad):
    length, vis = norm.shape[1], w_qkv.shape[0]
    bf16, f32 = jnp.bfloat16, jnp.float32
    vmem = pl.BlockSpec(memory_space=pltpu.VMEM)
    return pl.pallas_call(
        encoder_backward_kernel,
        out_shape=jax.ShapeDtypeStruct((length, vis), bf16),
        in_specs=[pl.BlockSpec(memory_space=pltpu.SMEM)]
        + [vmem] * 6
        + [pl.BlockSpec(memory_space=pltpu.HBM)],
        out_specs=vmem,
        scratch_shapes=[
            pltpu.VMEM((6, vis, CHUNK), bf16),
            pltpu.VMEM((2, length, CHUNK), f32),
            pltpu.VMEM((3, length, CHUNK), f32),
            pltpu.SemaphoreType.DMA((6,)),
        ],
        compiler_params=pltpu.CompilerParams(vmem_limit_bytes=40 << 20),
        cost_estimate=pl.CostEstimate(flops=1000, transcendentals=0, bytes_accessed=1000),
        name="encoder_backward",
    )(flag, grad, ln_gain, qkv, probs, norm, inverse, in_hbm(w_qkv))


def give_columns_kernel(start, flag_ref, after_ref, w_hbm, out_ref, sem):
    @pl.when(flag_ref[0] == 0)
    def _():
        copy = pltpu.make_async_copy(w_hbm.at[:, pl.ds(start, out_ref.shape[1])], out_ref, sem)
        copy.start()
        copy.wait()


def give_columns(flag, after, matrix, start, size):
    return pl.pallas_call(
        lambda *refs: give_columns_kernel(start, *refs),
        out_shape=jax.ShapeDtypeStruct((matrix.shape[0], size), matrix.dtype),
        in_specs=[
            pl.BlockSpec(memory_space=pltpu.SMEM),
            pl.BlockSpec(memory_space=pl.ANY),
            pl.BlockSpec(memory_space=pltpu.HBM),
        ],
        out_specs=pl.BlockSpec(memory_space=pltpu.VMEM),
        scratch_shapes=[pltpu.SemaphoreType.DMA],
        compiler_params=pltpu.CompilerParams(vmem_limit_bytes=16 << 20),
        cost_estimate=pl.CostEstimate(flops=1000, transcendentals=0, bytes_accessed=1000),
        name="give_columns",
    )(flag, after, in_hbm(matrix))


def give_cotangent_kernel(flag_ref, after_ref, gain_ref, cot_hbm, out_ref, sem):
    @pl.when(flag_ref[0] == 0)
    def _():
        rows, size = cot_hbm.shape[0], out_ref.shape[1]
        copy = pltpu.make_async_copy(
            cot_hbm.at[:, pl.ds(0, size)], out_ref.at[pl.ds(0, rows)], sem
        )
        copy.start()
        out_ref[rows:] = jnp.broadcast_to(gain_ref[:, :size], (GAIN_ROWS, size))
        copy.wait()


def give_cotangent(flag, after, gain, cot, size):
    return pl.pallas_call(
        give_cotangent_kernel,
        out_shape=jax.ShapeDtypeStruct((cot.shape[0] + GAIN_ROWS, size), cot.dtype),
        in_specs=[
            pl.BlockSpec(memory_space=pltpu.SMEM),
            pl.BlockSpec(memory_space=pl.ANY),
            pl.BlockSpec(memory_space=pltpu.VMEM),
            pl.BlockSpec(memory_space=pltpu.HBM),
        ],
        out_specs=pl.BlockSpec(memory_space=pltpu.VMEM),
        scratch_shapes=[pltpu.SemaphoreType.DMA],
        compiler_params=pltpu.CompilerParams(vmem_limit_bytes=16 << 20),
        cost_estimate=pl.CostEstimate(flops=1000, transcendentals=0, bytes_accessed=1000),
        name="give_cotangent",
    )(flag, after, gain, in_hbm(cot))


def in_hbm(array):
    return pltpu.with_memory_space_constraint(array, pltpu.HBM)


def partial_kernel(start, flag_ref, x_ref, got_ref, mine_ref, near_ref, late_ref, *refs):
    *homes, w_ref, sem = refs
    size = w_ref.shape[1]

    @pl.when(flag_ref[0] == 1)
    def _():
        copy = pltpu.make_async_copy(got_ref, w_ref, sem)
        copy.start()
        copy.wait()

    @pl.when(flag_ref[0] == 0)
    def _():
        copy = pltpu.make_async_copy(mine_ref.at[:, pl.ds(start, size)], w_ref, sem)
        copy.start()
        copy.wait()

    pairs, _, rows, depth = x_ref.shape
    weight = w_ref[...]
    away = dot(x_ref[:, 1].reshape(pairs * rows, depth), weight, NN)
    away = [away[s * rows : (s + 1) * rows].astype(near_ref.dtype) for s in range(pairs)]
    for i, s in enumerate(near_blocks(pairs)):
        near_ref[i] = away[s]
    for i, s in enumerate(late_blocks(pairs)):
        late_ref[i] = away[s]
    home = dot(x_ref[:, 0].reshape(pairs * rows, depth), weight, NN)
    for s in range(pairs):
        homes[s][...] = home[s * rows : (s + 1) * rows]


def near_blocks(pairs):
    return list(range(1, pairs // 2 + 1))


def late_blocks(pairs):
    return list(range(pairs // 2 + 1, pairs)) + [0]


def partial_products(flag, features, got, matrix, start):
    pairs, _, rows, depth = features.shape
    size = got.shape[1]
    vmem = pl.BlockSpec(memory_space=pltpu.VMEM)
    half = jax.ShapeDtypeStruct((pairs // 2, rows, size), jnp.bfloat16)
    near, late, *home, weight = pl.pallas_call(
        lambda *refs: partial_kernel(start, *refs),
        out_shape=(half, half)
        + (jax.ShapeDtypeStruct((rows, size), jnp.float32),) * pairs
        + (jax.ShapeDtypeStruct((depth, size), got.dtype),),
        in_specs=[
            pl.BlockSpec(memory_space=pltpu.SMEM),
            vmem,
            pl.BlockSpec(memory_space=pl.ANY),
            pl.BlockSpec(memory_space=pltpu.HBM),
        ],
        out_specs=(vmem,) * (3 + pairs),
        scratch_shapes=[pltpu.SemaphoreType.DMA],
        compiler_params=pltpu.CompilerParams(vmem_limit_bytes=32 << 20),
        cost_estimate=pl.CostEstimate(flops=1000, transcendentals=0, bytes_accessed=1000),
        name="partial_products",
    )(flag, features, in_hbm(got), in_hbm(matrix))
    return near, late, home, weight


def arrange_in_kernel(flag_ref, order_ref, a_ref, b_ref, out_ref):
    keep = flag_ref[0] == 1
    for r in range(out_ref.shape[0]):
        place = order_ref[r]
        out_ref[r] = jnp.where(keep, a_ref[place], b_ref[place])


def arrange_out_kernel(order_ref, a_ref, b_ref, out_ref):
    for r in range(out_ref.shape[0]):
        value = a_ref[r].astype(jnp.float32) + b_ref[r].astype(jnp.float32)
        out_ref[order_ref[r]] = value.astype(out_ref.dtype)


def arrange(kernel, name, scalars, a, b):
    vmem = pl.BlockSpec(memory_space=pltpu.VMEM)
    return pl.pallas_call(
        kernel,
        out_shape=jax.ShapeDtypeStruct(b.shape, b.dtype),
        in_specs=[pl.BlockSpec(memory_space=pltpu.SMEM)] * len(scalars) + [vmem, vmem],
        out_specs=vmem,
        compiler_params=pltpu.CompilerParams(vmem_limit_bytes=32 << 20),
        name=name,
    )(*scalars, a, b)


def passed_along(block, axis, distance):
    devices = range(lax.axis_size(axis))
    route = [(i - distance, i) for i in devices if i - distance in devices]
    return lax.ppermute(block, axis, route)


def rotated(blocks, shift):
    count = blocks.shape[0]
    step = 1
    while step < count:
        turned = jnp.concatenate([blocks[step:], blocks[:step]], axis=0)
        blocks = jnp.where((shift // step) % 2 == 1, turned, blocks)
        step *= 2
    return blocks


def sent_round(block, move):
    count = lax.axis_size("dp")
    return lax.ppermute(block, "dp", [(i, i ^ (2 * move)) for i in range(count)])


def sent_across(block):
    return lax.ppermute(block, "dp", [(i, i ^ 1) for i in range(lax.axis_size("dp"))])


def sent_tp(block, distance):
    count = lax.axis_size("tp")
    return lax.ppermute(block, "tp", [(i, (i + distance) % count) for i in range(count)])


def per_device(frames, counts, w_qkv, ln_gain, w_proj, rms_gain, cotangent):
    f32, bf16 = jnp.float32, jnp.bfloat16
    is_encoder = lax.axis_index("grp") == 0
    flag = is_encoder.astype(jnp.int32).reshape(1)
    dp_count, tp_count = lax.axis_size("dp"), lax.axis_size("tp")
    pair_count = dp_count // 2
    dp_index, tp_index = lax.axis_index("dp"), lax.axis_index("tp")
    relative = jnp.arange(dp_count, dtype=jnp.int32)
    order = dp_index ^ relative

    frame = frames[0, 0]
    tokens_here = frame.shape[0] // 4
    depth = w_proj.shape[1]
    half = w_proj.shape[2] // 2
    first = half * FIRST_PART // 16 // 128 * 128
    sizes = (first, half - first)

    w_mine, cot_mine = w_proj[0], cotangent[0]
    give = [give_columns(flag, flag, w_mine, 0, sizes[0])]
    give.append(give_columns(flag, give[0], w_mine, first, sizes[1]))
    got = [passed_along(block, "grp", -1) for block in give]
    got_cot = passed_along(give_cotangent(flag, give[1], rms_gain, cot_mine, half), "grp", -1)

    embedded, qkv, probs, norm, inverse = encoder_forward(flag, frame, w_qkv[0], ln_gain)

    pieces = embedded
    if depth != CHUNK:
        pieces = embedded.reshape(-1, tokens_here, CHUNK // depth, depth)
        pieces = pieces.transpose(0, 2, 1, 3).reshape(dp_count, tokens_here, depth)
    swapped = lax.all_to_all(pieces, "dp", 0, 0)
    arrived = passed_along(swapped, "grp", 1)
    features = arrange(arrange_in_kernel, "arrange_in", (flag, order), swapped, arrived)
    features = jnp.concatenate(
        [features] + [sent_tp(features, tp_count - s) for s in range(1, tp_count)], axis=1
    ).reshape(pair_count, 2, tp_count * tokens_here, depth)

    acts, weights = [], []
    for c in range(2):
        near, late, home, weight = partial_products(flag, features, got[c], w_mine, half + c * first)
        weights.append(weight)
        near, late = sent_across(near), sent_across(late)
        for i, s in enumerate(near_blocks(pair_count)):
            home[s] = home[s] + near[i].astype(f32)
        for i, s in enumerate(late_blocks(pair_count)):
            home[s] = home[s] + late[i].astype(f32)
        sends = [block.astype(bf16) for block in home[1:]]
        if c == 0:
            sends, features = lax.optimization_barrier((sends, features))
        total = home[0]
        for s, block in enumerate(sends):
            total = total + sent_round(block, s + 1).astype(f32)
        acts.append(total)

    got_cot, acts[0] = lax.optimization_barrier((got_cot, acts[0]))
    rows = cot_mine.shape[0]
    cot = jnp.where(is_encoder, got_cot[:rows], cot_mine[:, half:])
    gain_rms = jnp.where(is_encoder, got_cot[rows : rows + 1], rms_gain[:, half:])
    slot = lax.broadcasted_iota(jnp.int32, (1, tokens_here), 1) // TOKF
    live_mask = (slot < rotated(counts, tp_index)[:, None]).astype(f32).reshape(-1, 1)
    cot = rotated(cot.reshape(tp_count, tokens_here, half), tp_index).reshape(-1, half)
    scaled = gain_rms.astype(f32) * cot.astype(f32) * live_mask
    scaled = (scaled[:, :first], scaled[:, first:])
    squares = sum(jnp.sum(act * act, axis=1) for act in acts)
    products = sum(jnp.sum(act * part, axis=1) for act, part in zip(acts, scaled))
    sums = jnp.stack([squares, products], axis=1).reshape(tp_count, tokens_here, 2)
    sums = lax.psum(rotated(sums, (tp_count - tp_index) % tp_count), ("grp", "tp"))
    sums = rotated(sums, tp_index).reshape(-1, 2)
    inverse_rms = lax.rsqrt(sums[:, :1] / D + 1e-06)
    fall = inverse_rms**3 * (sums[:, 1:] / D)
    grads = [
        (inverse_rms * part - act * fall).astype(bf16) for act, part in zip(acts, scaled)
    ]

    def gathered_round(block):
        blocks = [block] + [None] * (pair_count - 1)
        for s in range(1, pair_count):
            blocks[s] = sent_round(block, s)
        return jnp.stack(blocks)

    near = gathered_round(grads[0])
    duo = jnp.stack([grads[1], sent_across(grads[1])])
    near, duo = lax.optimization_barrier((near, duo))
    far = sent_across(near)
    duos = gathered_round(duo)
    near, far = (near, duos[:, 0]), (far, duos[:, 1])

    def back(blocks):
        return sum(
            jnp.einsum("prc,kc->prk", block, weight, preferred_element_type=f32)
            for block, weight in zip(blocks, weights)
        )

    terms = [back(near), back(far)]
    terms = jnp.stack(
        [term.reshape(pair_count, tp_count, tokens_here, depth) for term in terms], axis=1
    ).reshape(dp_count, tp_count, tokens_here, depth)
    total = terms[:, 0]
    for s in range(1, tp_count):
        total = total + sent_tp(terms[:, s].astype(bf16), s).astype(f32)
    total = total.astype(bf16)
    returned = passed_along(total, "grp", -1)
    whole = arrange(arrange_out_kernel, "arrange_out", (order,), total, returned)
    whole = lax.all_to_all(whole, "dp", 0, 0)
    if depth != CHUNK:
        whole = whole.reshape(-1, CHUNK // depth, tokens_here, depth)
        whole = whole.transpose(0, 2, 1, 3).reshape(-1, tokens_here, CHUNK)

    grad_frames = encoder_backward(flag, w_qkv[0], ln_gain, qkv, probs, norm, inverse, whole)
    return grad_frames[None, None]


def solution(mesh):
    placed = (
        P("grp", ("dp", "tp"), None, None),
        P("dp"),
        P("grp", None, None),
        P("grp", None),
        P("grp", "dp", "tp"),
        P("grp", "tp"),
        P("grp", "dp", "tp"),
    )
    return jax.shard_map(
        per_device,
        mesh=mesh,
        in_specs=placed,
        out_specs=P("grp", ("dp", "tp"), None, None),
        check_vma=False,
    )
```

```python
import jax
import jax.numpy as jnp
from jax import lax
from jax.experimental import pallas as pl
from jax.experimental.pallas import tpu as pltpu
from jax.sharding import PartitionSpec as P

HEADS = 16
HDIM = 80
D = 8192
TOKF = 32
FIRST_PART = 9
GAIN_ROWS = 16
CHUNK = 640
CHUNK_HEADS = CHUNK // HDIM


def head_window(head):
    low, high = head * HDIM, (head + 1) * HDIM
    start, stop = low // 128 * 128, -(-high // 128) * 128
    return start, stop, low - start, high - start


def head_only(block, low, high):
    lane = lax.broadcasted_iota(jnp.int32, block.shape, 1)
    return jnp.where((lane >= low) & (lane < high), block, jnp.zeros_like(block))


def dot(a, b, dims):
    return lax.dot_general(a, b, (dims, ((), ())), preferred_element_type=jnp.float32)


def add_tiles(tiles, block, start):
    for i in range(block.shape[1] // 128):
        tile = start // 128 + i
        part = block[:, i * 128 : (i + 1) * 128]
        tiles[tile] = part if tile not in tiles else tiles[tile] + part


NT = ((1,), (1,))
NN = ((1,), (0,))
TN = ((0,), (0,))


def token_order(length):
    row = lax.broadcasted_iota(jnp.int32, (length, length), 0)
    column = lax.broadcasted_iota(jnp.int32, (length, length), 1)
    tokens = length // 4
    return (row % tokens * 4 + row // tokens == column).astype(jnp.bfloat16)


def weight_copies(w_hbm, w_buf, sems):
    return [
        pltpu.make_async_copy(
            w_hbm.at[:, pl.ds(((i % 3) * 2 + i // 3) * CHUNK, CHUNK)], w_buf.at[i], sems.at[i]
        )
        for i in range(6)
    ]


def encoder_forward_kernel(
    flag_ref,
    x_ref,
    gain_ref,
    w_hbm,
    emb_ref,
    qkv_hbm,
    probs_hbm,
    norm_hbm,
    inv_ref,
    w_buf,
    qkv_ref,
    probs_ref,
    norm_ref,
    work,
    sems,
    out_sems,
):
    @pl.when(flag_ref[0] == 1)
    def _():
        copies = weight_copies(w_hbm, w_buf, sems)
        for copy in copies:
            copy.start()
        outs = []
        x = x_ref[...]
        vis = x.shape[1]
        for half in range(2):
            for kind in range(3):
                i = half * 3 + kind
                copies[i].wait()
                qkv_ref[i] = dot(x, w_buf[i], NN).astype(jnp.bfloat16)
            heads = pl.ds(half * CHUNK_HEADS, CHUNK_HEADS)
            outs.append(
                pltpu.make_async_copy(
                    qkv_ref.at[pl.ds(half * 3, 3)],
                    qkv_hbm.at[pl.ds(half * 3, 3)],
                    out_sems.at[half],
                )
            )
            outs[-1].start()
            tiles = {}
            add_tiles(tiles, x[:, half * CHUNK : (half + 1) * CHUNK].astype(jnp.float32), 0)
            for head in range(CHUNK_HEADS):
                start, stop, low, high = head_window(head)
                query = qkv_ref[half * 3, :, start:stop]
                key = head_only(qkv_ref[half * 3 + 1, :, start:stop], low, high)
                value = head_only(qkv_ref[half * 3 + 2, :, start:stop], low, high)
                scores = dot(query, key, NT) * HDIM ** (-0.5)
                weights = jnp.exp(scores - jnp.max(scores, axis=1, keepdims=True))
                weights = weights / jnp.sum(weights, axis=1, keepdims=True)
                probs_ref[half * CHUNK_HEADS + head] = weights
                add_tiles(tiles, dot(weights.astype(jnp.bfloat16), value, NN), start)
            for tile, part in tiles.items():
                work[half, :, tile * 128 : (tile + 1) * 128] = part
            outs.append(
                pltpu.make_async_copy(probs_ref.at[heads], probs_hbm.at[heads], out_sems.at[2 + half])
            )
            outs[-1].start()
        first, second = work[0], work[1]
        mean = (
            jnp.sum(first, axis=1, keepdims=True) + jnp.sum(second, axis=1, keepdims=True)
        ) / vis
        first, second = first - mean, second - mean
        variance = (
            jnp.sum(first * first, axis=1, keepdims=True)
            + jnp.sum(second * second, axis=1, keepdims=True)
        ) / vis
        inverse = lax.rsqrt(variance + 1e-06)
        inv_ref[...] = inverse
        gain = gain_ref[...].astype(jnp.float32)
        tokens = x.shape[0] // 4
        order = token_order(x.shape[0])
        for half, centred in enumerate((first, second)):
            normal = centred * inverse
            norm_ref[half] = normal
            embedded = (normal * gain[:, half * CHUNK : (half + 1) * CHUNK]).astype(jnp.bfloat16)
            embedded = dot(order, embedded, NN).astype(jnp.bfloat16)
            for j in range(4):
                emb_ref[j * 2 + half] = embedded[j * tokens : (j + 1) * tokens]
        outs.append(pltpu.make_async_copy(norm_ref, norm_hbm, out_sems.at[4]))
        outs[-1].start()
        for copy in outs:
            copy.wait()


def encoder_forward(flag, frame, w_qkv, ln_gain):
    length, vis = frame.shape
    bf16, f32 = jnp.bfloat16, jnp.float32
    vmem = pl.BlockSpec(memory_space=pltpu.VMEM)
    hbm = pl.BlockSpec(memory_space=pltpu.HBM)
    return pl.pallas_call(
        encoder_forward_kernel,
        out_shape=(
            jax.ShapeDtypeStruct((8, length // 4, CHUNK), bf16),
            pltpu.HBM((6, length, CHUNK), bf16),
            pltpu.HBM((HEADS, length, length), f32),
            pltpu.HBM((2, length, CHUNK), f32),
            jax.ShapeDtypeStruct((length, 1), f32),
        ),
        in_specs=[pl.BlockSpec(memory_space=pltpu.SMEM), vmem, vmem, hbm],
        out_specs=(vmem, hbm, hbm, hbm, vmem),
        scratch_shapes=[
            pltpu.VMEM((6, vis, CHUNK), bf16),
            pltpu.VMEM((6, length, CHUNK), bf16),
            pltpu.VMEM((HEADS, length, length), f32),
            pltpu.VMEM((2, length, CHUNK), f32),
            pltpu.VMEM((2, length, CHUNK), f32),
            pltpu.SemaphoreType.DMA((6,)),
            pltpu.SemaphoreType.DMA((5,)),
        ],
        compiler_params=pltpu.CompilerParams(vmem_limit_bytes=40 << 20),
        cost_estimate=pl.CostEstimate(flops=1000, transcendentals=0, bytes_accessed=1000),
        name="encoder_forward",
    )(flag, frame, ln_gain, in_hbm(w_qkv))


def encoder_backward_kernel(
    flag_ref,
    grad_ref,
    gain_ref,
    qkv_ref,
    probs_ref,
    norm_ref,
    inv_ref,
    w_hbm,
    out_ref,
    w_buf,
    work,
    mix,
    sems,
):
    @pl.when(flag_ref[0] == 0)
    def _():
        out_ref[...] = jnp.zeros_like(out_ref)

    @pl.when(flag_ref[0] == 1)
    def _():
        f32, bf16 = jnp.float32, jnp.bfloat16
        copies = weight_copies(w_hbm, w_buf, sems)
        for copy in copies:
            copy.start()
        vis = w_hbm.shape[0]
        tokens = grad_ref.shape[1]
        gain = gain_ref[...].astype(f32)
        order = token_order(4 * tokens)
        for half in range(2):
            grads = jnp.concatenate([grad_ref[j * 2 + half] for j in range(4)], axis=0)
            work[half] = dot(order, grads, TN) * gain[:, half * CHUNK : (half + 1) * CHUNK]
        mean = (
            jnp.sum(work[0], axis=1, keepdims=True) + jnp.sum(work[1], axis=1, keepdims=True)
        ) / vis
        along = (
            jnp.sum(work[0] * norm_ref[0], axis=1, keepdims=True)
            + jnp.sum(work[1] * norm_ref[1], axis=1, keepdims=True)
        ) / vis
        inverse = inv_ref[...]
        for half in range(2):
            work[half] = inverse * (work[half] - mean - norm_ref[half] * along)
        total = jnp.zeros((work.shape[1], vis), f32)
        for half in range(2):
            mixed = [{}, {}, {}]
            for head in range(CHUNK_HEADS):
                start, stop, low, high = head_window(head)
                grad = head_only(work[half, :, start:stop].astype(bf16), low, high)
                query = head_only(qkv_ref[half * 3, :, start:stop], low, high)
                key = head_only(qkv_ref[half * 3 + 1, :, start:stop], low, high)
                value = qkv_ref[half * 3 + 2, :, start:stop]
                probs = probs_ref[half * CHUNK_HEADS + head]
                grad_weights = dot(grad, value, NT)
                inner = jnp.sum(grad_weights * probs, axis=1, keepdims=True)
                scores = (probs * (grad_weights - inner) * HDIM ** (-0.5)).astype(bf16)
                add_tiles(mixed[2], dot(probs.astype(bf16), grad, TN), start)
                add_tiles(mixed[0], dot(scores, key, NN), start)
                add_tiles(mixed[1], dot(scores, query, TN), start)
            for kind in range(3):
                for tile, part in mixed[kind].items():
                    mix[kind, :, tile * 128 : (tile + 1) * 128] = part.astype(bf16)
            for kind in range(3):
                i = half * 3 + kind
                copies[i].wait()
                total = total + dot(mix[kind], w_buf[i], NT)
        for half in range(2):
            columns = slice(half * CHUNK, (half + 1) * CHUNK)
            out_ref[:, columns] = (work[half] + total[:, columns]).astype(bf16)


def encoder_backward(flag, w_qkv, ln_gain, qkv, probs, norm, inverse, grad):
    length, vis = norm.shape[1], w_qkv.shape[0]
    bf16, f32 = jnp.bfloat16, jnp.float32
    vmem = pl.BlockSpec(memory_space=pltpu.VMEM)
    return pl.pallas_call(
        encoder_backward_kernel,
        out_shape=jax.ShapeDtypeStruct((length, vis), bf16),
        in_specs=[pl.BlockSpec(memory_space=pltpu.SMEM)]
        + [vmem] * 6
        + [pl.BlockSpec(memory_space=pltpu.HBM)],
        out_specs=vmem,
        scratch_shapes=[
            pltpu.VMEM((6, vis, CHUNK), bf16),
            pltpu.VMEM((2, length, CHUNK), f32),
            pltpu.VMEM((3, length, CHUNK), bf16),
            pltpu.SemaphoreType.DMA((6,)),
        ],
        compiler_params=pltpu.CompilerParams(vmem_limit_bytes=40 << 20),
        cost_estimate=pl.CostEstimate(flops=1000, transcendentals=0, bytes_accessed=1000),
        name="encoder_backward",
    )(flag, grad, ln_gain, qkv, probs, norm, inverse, in_hbm(w_qkv))


def give_columns_kernel(start, flag_ref, after_ref, w_hbm, out_ref, sem):
    @pl.when(flag_ref[0] == 0)
    def _():
        copy = pltpu.make_async_copy(w_hbm.at[:, pl.ds(start, out_ref.shape[1])], out_ref, sem)
        copy.start()
        copy.wait()


def give_columns(flag, after, matrix, start, size):
    return pl.pallas_call(
        lambda *refs: give_columns_kernel(start, *refs),
        out_shape=jax.ShapeDtypeStruct((matrix.shape[0], size), matrix.dtype),
        in_specs=[
            pl.BlockSpec(memory_space=pltpu.SMEM),
            pl.BlockSpec(memory_space=pl.ANY),
            pl.BlockSpec(memory_space=pltpu.HBM),
        ],
        out_specs=pl.BlockSpec(memory_space=pltpu.VMEM),
        scratch_shapes=[pltpu.SemaphoreType.DMA],
        compiler_params=pltpu.CompilerParams(vmem_limit_bytes=16 << 20),
        cost_estimate=pl.CostEstimate(flops=1000, transcendentals=0, bytes_accessed=1000),
        name="give_columns",
    )(flag, after, in_hbm(matrix))


def give_cotangent_kernel(flag_ref, after_ref, gain_ref, cot_hbm, out_ref, sem):
    @pl.when(flag_ref[0] == 0)
    def _():
        rows, size = cot_hbm.shape[0], out_ref.shape[1]
        copy = pltpu.make_async_copy(
            cot_hbm.at[:, pl.ds(0, size)], out_ref.at[pl.ds(0, rows)], sem
        )
        copy.start()
        out_ref[rows:] = jnp.broadcast_to(gain_ref[:, :size], (GAIN_ROWS, size))
        copy.wait()


def give_cotangent(flag, after, gain, cot, size):
    return pl.pallas_call(
        give_cotangent_kernel,
        out_shape=jax.ShapeDtypeStruct((cot.shape[0] + GAIN_ROWS, size), cot.dtype),
        in_specs=[
            pl.BlockSpec(memory_space=pltpu.SMEM),
            pl.BlockSpec(memory_space=pl.ANY),
            pl.BlockSpec(memory_space=pltpu.VMEM),
            pl.BlockSpec(memory_space=pltpu.HBM),
        ],
        out_specs=pl.BlockSpec(memory_space=pltpu.VMEM),
        scratch_shapes=[pltpu.SemaphoreType.DMA],
        compiler_params=pltpu.CompilerParams(vmem_limit_bytes=16 << 20),
        cost_estimate=pl.CostEstimate(flops=1000, transcendentals=0, bytes_accessed=1000),
        name="give_cotangent",
    )(flag, after, gain, in_hbm(cot))


def in_hbm(array):
    return pltpu.with_memory_space_constraint(array, pltpu.HBM)


def partial_kernel(start, flag_ref, x_ref, got_ref, mine_ref, near_ref, late_ref, *refs):
    *homes, w_ref, sem = refs
    size = w_ref.shape[1]

    @pl.when(flag_ref[0] == 1)
    def _():
        copy = pltpu.make_async_copy(got_ref, w_ref, sem)
        copy.start()
        copy.wait()

    @pl.when(flag_ref[0] == 0)
    def _():
        copy = pltpu.make_async_copy(mine_ref.at[:, pl.ds(start, size)], w_ref, sem)
        copy.start()
        copy.wait()

    pairs, _, rows, depth = x_ref.shape
    weight = w_ref[...]
    away = dot(x_ref[:, 1].reshape(pairs * rows, depth), weight, NN)
    away = [away[s * rows : (s + 1) * rows].astype(near_ref.dtype) for s in range(pairs)]
    for i, s in enumerate(near_blocks(pairs)):
        near_ref[i] = away[s]
    for i, s in enumerate(late_blocks(pairs)):
        late_ref[i] = away[s]
    home = dot(x_ref[:, 0].reshape(pairs * rows, depth), weight, NN)
    for s in range(pairs):
        homes[s][...] = home[s * rows : (s + 1) * rows]


def near_blocks(pairs):
    return list(range(1, pairs // 2 + 1))


def late_blocks(pairs):
    return list(range(pairs // 2 + 1, pairs)) + [0]


def partial_products(flag, features, got, matrix, start):
    pairs, _, rows, depth = features.shape
    size = got.shape[1]
    vmem = pl.BlockSpec(memory_space=pltpu.VMEM)
    half = jax.ShapeDtypeStruct((pairs // 2, rows, size), jnp.bfloat16)
    near, late, *home, weight = pl.pallas_call(
        lambda *refs: partial_kernel(start, *refs),
        out_shape=(half, half)
        + (jax.ShapeDtypeStruct((rows, size), jnp.float32),) * pairs
        + (jax.ShapeDtypeStruct((depth, size), got.dtype),),
        in_specs=[
            pl.BlockSpec(memory_space=pltpu.SMEM),
            vmem,
            pl.BlockSpec(memory_space=pl.ANY),
            pl.BlockSpec(memory_space=pltpu.HBM),
        ],
        out_specs=(vmem,) * (3 + pairs),
        scratch_shapes=[pltpu.SemaphoreType.DMA],
        compiler_params=pltpu.CompilerParams(vmem_limit_bytes=32 << 20),
        cost_estimate=pl.CostEstimate(flops=1000, transcendentals=0, bytes_accessed=1000),
        name="partial_products",
    )(flag, features, in_hbm(got), in_hbm(matrix))
    return near, late, home, weight


def arrange_in_kernel(flag_ref, order_ref, a_ref, b_ref, out_ref):
    keep = flag_ref[0] == 1
    for r in range(out_ref.shape[0]):
        place = order_ref[r]
        out_ref[r] = jnp.where(keep, a_ref[place], b_ref[place])


def arrange_out_kernel(order_ref, a_ref, b_ref, out_ref):
    for r in range(out_ref.shape[0]):
        value = a_ref[r].astype(jnp.float32) + b_ref[r].astype(jnp.float32)
        out_ref[order_ref[r]] = value.astype(out_ref.dtype)


def arrange(kernel, name, scalars, a, b):
    vmem = pl.BlockSpec(memory_space=pltpu.VMEM)
    return pl.pallas_call(
        kernel,
        out_shape=jax.ShapeDtypeStruct(b.shape, b.dtype),
        in_specs=[pl.BlockSpec(memory_space=pltpu.SMEM)] * len(scalars) + [vmem, vmem],
        out_specs=vmem,
        compiler_params=pltpu.CompilerParams(vmem_limit_bytes=32 << 20),
        name=name,
    )(*scalars, a, b)


def passed_along(block, axis, distance):
    devices = range(lax.axis_size(axis))
    route = [(i - distance, i) for i in devices if i - distance in devices]
    return lax.ppermute(block, axis, route)


def rotated(blocks, shift):
    count = blocks.shape[0]
    step = 1
    while step < count:
        turned = jnp.concatenate([blocks[step:], blocks[:step]], axis=0)
        blocks = jnp.where((shift // step) % 2 == 1, turned, blocks)
        step *= 2
    return blocks


def sent_round(block, move):
    count = lax.axis_size("dp")
    return lax.ppermute(block, "dp", [(i, i ^ (2 * move)) for i in range(count)])


def sent_across(block):
    return lax.ppermute(block, "dp", [(i, i ^ 1) for i in range(lax.axis_size("dp"))])


def sent_tp(block, distance):
    count = lax.axis_size("tp")
    return lax.ppermute(block, "tp", [(i, (i + distance) % count) for i in range(count)])


def per_device(frames, counts, w_qkv, ln_gain, w_proj, rms_gain, cotangent):
    f32, bf16 = jnp.float32, jnp.bfloat16
    is_encoder = lax.axis_index("grp") == 0
    flag = is_encoder.astype(jnp.int32).reshape(1)
    dp_count, tp_count = lax.axis_size("dp"), lax.axis_size("tp")
    pair_count = dp_count // 2
    dp_index, tp_index = lax.axis_index("dp"), lax.axis_index("tp")
    relative = jnp.arange(dp_count, dtype=jnp.int32)
    order = dp_index ^ relative

    frame = frames[0, 0]
    tokens_here = frame.shape[0] // 4
    depth = w_proj.shape[1]
    half = w_proj.shape[2] // 2
    first = half * FIRST_PART // 16 // 128 * 128
    sizes = (first, half - first)

    w_mine, cot_mine = w_proj[0], cotangent[0]
    give = [give_columns(flag, flag, w_mine, 0, sizes[0])]
    give.append(give_columns(flag, give[0], w_mine, first, sizes[1]))
    got = [passed_along(block, "grp", -1) for block in give]
    give_cot = give_cotangent(flag, give[1], rms_gain, cot_mine, half)

    embedded, qkv, probs, norm, inverse = encoder_forward(flag, frame, w_qkv[0], ln_gain)

    pieces = embedded
    if depth != CHUNK:
        pieces = embedded.reshape(-1, tokens_here, CHUNK // depth, depth)
        pieces = pieces.transpose(0, 2, 1, 3).reshape(dp_count, tokens_here, depth)
    swapped = lax.all_to_all(pieces, "dp", 0, 0)
    arrived = passed_along(swapped, "grp", 1)
    swapped, give_cot = lax.optimization_barrier((swapped, give_cot))
    got_cot = passed_along(give_cot, "grp", -1)
    features = arrange(arrange_in_kernel, "arrange_in", (flag, order), swapped, arrived)
    features = jnp.concatenate(
        [features] + [sent_tp(features, tp_count - s) for s in range(1, tp_count)], axis=1
    ).reshape(pair_count, 2, tp_count * tokens_here, depth)

    acts, weights = [], []
    for c in range(2):
        near, late, home, weight = partial_products(flag, features, got[c], w_mine, half + c * first)
        weights.append(weight)
        near, late = sent_across(near), sent_across(late)
        for i, s in enumerate(near_blocks(pair_count)):
            home[s] = home[s] + near[i].astype(f32)
        for i, s in enumerate(late_blocks(pair_count)):
            home[s] = home[s] + late[i].astype(f32)
        sends = [block.astype(bf16) for block in home[1:]]
        if c == 0:
            sends, features = lax.optimization_barrier((sends, features))
        total = home[0]
        for s, block in enumerate(sends):
            total = total + sent_round(block, s + 1).astype(f32)
        acts.append(total)

    got_cot, acts[0] = lax.optimization_barrier((got_cot, acts[0]))
    rows = cot_mine.shape[0]
    cot = jnp.where(is_encoder, got_cot[:rows], cot_mine[:, half:])
    gain_rms = jnp.where(is_encoder, got_cot[rows : rows + 1], rms_gain[:, half:])
    slot = lax.broadcasted_iota(jnp.int32, (1, tokens_here), 1) // TOKF
    live_mask = (slot < rotated(counts, tp_index)[:, None]).astype(f32).reshape(-1, 1)
    cot = rotated(cot.reshape(tp_count, tokens_here, half), tp_index).reshape(-1, half)
    scaled = gain_rms.astype(f32) * cot.astype(f32) * live_mask
    scaled = (scaled[:, :first], scaled[:, first:])
    squares = sum(jnp.sum(act * act, axis=1) for act in acts)
    products = sum(jnp.sum(act * part, axis=1) for act, part in zip(acts, scaled))
    sums = jnp.stack([squares, products], axis=1).reshape(tp_count, tokens_here, 2)
    sums = lax.psum(rotated(sums, (tp_count - tp_index) % tp_count), ("grp", "tp"))
    sums = rotated(sums, tp_index).reshape(-1, 2)
    inverse_rms = lax.rsqrt(sums[:, :1] / D + 1e-06)
    fall = inverse_rms**3 * (sums[:, 1:] / D)
    grads = [
        (inverse_rms * part - act * fall).astype(bf16) for act, part in zip(acts, scaled)
    ]

    def gathered_round(block):
        blocks = [block] + [None] * (pair_count - 1)
        for s in range(1, pair_count):
            blocks[s] = sent_round(block, s)
        return jnp.stack(blocks)

    near = gathered_round(grads[0])
    duo = jnp.stack([grads[1], sent_across(grads[1])])
    near, duo = lax.optimization_barrier((near, duo))
    far = sent_across(near)
    duos = gathered_round(duo)
    near, far = (near, duos[:, 0]), (far, duos[:, 1])

    def back(blocks):
        return sum(
            jnp.einsum("prc,kc->prk", block, weight, preferred_element_type=f32)
            for block, weight in zip(blocks, weights)
        )

    terms = [back(near), back(far)]
    terms = jnp.stack(
        [term.reshape(pair_count, tp_count, tokens_here, depth) for term in terms], axis=1
    ).reshape(dp_count, tp_count, tokens_here, depth)
    total = terms[:, 0]
    for s in range(1, tp_count):
        total = total + sent_tp(terms[:, s].astype(bf16), s).astype(f32)
    total = total.astype(bf16)
    returned = passed_along(total, "grp", -1)
    whole = arrange(arrange_out_kernel, "arrange_out", (order,), total, returned)
    whole = lax.all_to_all(whole, "dp", 0, 0)
    if depth != CHUNK:
        whole = whole.reshape(-1, CHUNK // depth, tokens_here, depth)
        whole = whole.transpose(0, 2, 1, 3).reshape(-1, tokens_here, CHUNK)

    grad_frames = encoder_backward(flag, w_qkv[0], ln_gain, qkv, probs, norm, inverse, whole)
    return grad_frames[None, None]


def solution(mesh):
    placed = (
        P("grp", ("dp", "tp"), None, None),
        P("dp"),
        P("grp", None, None),
        P("grp", None),
        P("grp", "dp", "tp"),
        P("grp", "tp"),
        P("grp", "dp", "tp"),
    )
    return jax.shard_map(
        per_device,
        mesh=mesh,
        in_specs=placed,
        out_specs=P("grp", ("dp", "tp"), None, None),
        check_vma=False,
    )
```

```python
import jax
import jax.numpy as jnp
from jax import lax
from jax.experimental import pallas as pl
from jax.experimental.pallas import tpu as pltpu
from jax.sharding import PartitionSpec as P

HEADS = 16
HDIM = 80
D = 8192
TOKF = 32
FIRST_PART = 9
GAIN_ROWS = 16
CHUNK = 640
CHUNK_HEADS = CHUNK // HDIM


def head_window(head):
    low, high = head * HDIM, (head + 1) * HDIM
    start, stop = low // 128 * 128, -(-high // 128) * 128
    return start, stop, low - start, high - start


def head_only(block, low, high):
    lane = lax.broadcasted_iota(jnp.int32, block.shape, 1)
    return jnp.where((lane >= low) & (lane < high), block, jnp.zeros_like(block))


def dot(a, b, dims):
    return lax.dot_general(a, b, (dims, ((), ())), preferred_element_type=jnp.float32)


def add_tiles(tiles, block, start):
    for i in range(block.shape[1] // 128):
        tile = start // 128 + i
        part = block[:, i * 128 : (i + 1) * 128]
        tiles[tile] = part if tile not in tiles else tiles[tile] + part


NT = ((1,), (1,))
NN = ((1,), (0,))
TN = ((0,), (0,))


def token_order(length):
    row = lax.broadcasted_iota(jnp.int32, (length, length), 0)
    column = lax.broadcasted_iota(jnp.int32, (length, length), 1)
    tokens = length // 4
    return (row % tokens * 4 + row // tokens == column).astype(jnp.bfloat16)


def weight_copies(w_hbm, w_buf, sems):
    return [
        pltpu.make_async_copy(
            w_hbm.at[:, pl.ds(((i % 3) * 2 + i // 3) * CHUNK, CHUNK)], w_buf.at[i], sems.at[i]
        )
        for i in range(6)
    ]


def encoder_forward_kernel(
    flag_ref,
    x_ref,
    gain_ref,
    w_hbm,
    emb_ref,
    qkv_hbm,
    probs_hbm,
    norm_hbm,
    inv_ref,
    w_buf,
    qkv_ref,
    probs_ref,
    norm_ref,
    work,
    sems,
    out_sems,
):
    @pl.when(flag_ref[0] == 1)
    def _():
        copies = weight_copies(w_hbm, w_buf, sems)
        for copy in copies:
            copy.start()
        outs = []
        x = x_ref[...]
        vis = x.shape[1]
        for half in range(2):
            for kind in range(3):
                i = half * 3 + kind
                copies[i].wait()
                qkv_ref[i] = dot(x, w_buf[i], NN).astype(jnp.bfloat16)
            heads = pl.ds(half * CHUNK_HEADS, CHUNK_HEADS)
            outs.append(
                pltpu.make_async_copy(
                    qkv_ref.at[pl.ds(half * 3, 3)],
                    qkv_hbm.at[pl.ds(half * 3, 3)],
                    out_sems.at[half],
                )
            )
            outs[-1].start()
            tiles = {}
            add_tiles(tiles, x[:, half * CHUNK : (half + 1) * CHUNK].astype(jnp.float32), 0)
            for head in range(CHUNK_HEADS):
                start, stop, low, high = head_window(head)
                query = qkv_ref[half * 3, :, start:stop]
                key = head_only(qkv_ref[half * 3 + 1, :, start:stop], low, high)
                value = head_only(qkv_ref[half * 3 + 2, :, start:stop], low, high)
                scores = dot(query, key, NT) * HDIM ** (-0.5)
                weights = jnp.exp(scores - jnp.max(scores, axis=1, keepdims=True))
                weights = weights / jnp.sum(weights, axis=1, keepdims=True)
                probs_ref[half * CHUNK_HEADS + head] = weights
                add_tiles(tiles, dot(weights.astype(jnp.bfloat16), value, NN), start)
            for tile, part in tiles.items():
                work[half, :, tile * 128 : (tile + 1) * 128] = part
            outs.append(
                pltpu.make_async_copy(probs_ref.at[heads], probs_hbm.at[heads], out_sems.at[2 + half])
            )
            outs[-1].start()
        first, second = work[0], work[1]
        mean = (
            jnp.sum(first, axis=1, keepdims=True) + jnp.sum(second, axis=1, keepdims=True)
        ) / vis
        first, second = first - mean, second - mean
        variance = (
            jnp.sum(first * first, axis=1, keepdims=True)
            + jnp.sum(second * second, axis=1, keepdims=True)
        ) / vis
        inverse = lax.rsqrt(variance + 1e-06)
        inv_ref[...] = inverse
        gain = gain_ref[...].astype(jnp.float32)
        tokens = x.shape[0] // 4
        order = token_order(x.shape[0])
        for half, centred in enumerate((first, second)):
            normal = centred * inverse
            norm_ref[half] = normal
            embedded = (normal * gain[:, half * CHUNK : (half + 1) * CHUNK]).astype(jnp.bfloat16)
            embedded = dot(order, embedded, NN).astype(jnp.bfloat16)
            for j in range(4):
                emb_ref[j * 2 + half] = embedded[j * tokens : (j + 1) * tokens]
        outs.append(pltpu.make_async_copy(norm_ref, norm_hbm, out_sems.at[4]))
        outs[-1].start()
        for copy in outs:
            copy.wait()


def encoder_forward(flag, frame, w_qkv, ln_gain):
    length, vis = frame.shape
    bf16, f32 = jnp.bfloat16, jnp.float32
    vmem = pl.BlockSpec(memory_space=pltpu.VMEM)
    hbm = pl.BlockSpec(memory_space=pltpu.HBM)
    return pl.pallas_call(
        encoder_forward_kernel,
        out_shape=(
            jax.ShapeDtypeStruct((8, length // 4, CHUNK), bf16),
            pltpu.HBM((6, length, CHUNK), bf16),
            pltpu.HBM((HEADS, length, length), f32),
            pltpu.HBM((2, length, CHUNK), f32),
            jax.ShapeDtypeStruct((length, 1), f32),
        ),
        in_specs=[pl.BlockSpec(memory_space=pltpu.SMEM), vmem, vmem, hbm],
        out_specs=(vmem, hbm, hbm, hbm, vmem),
        scratch_shapes=[
            pltpu.VMEM((6, vis, CHUNK), bf16),
            pltpu.VMEM((6, length, CHUNK), bf16),
            pltpu.VMEM((HEADS, length, length), f32),
            pltpu.VMEM((2, length, CHUNK), f32),
            pltpu.VMEM((2, length, CHUNK), f32),
            pltpu.SemaphoreType.DMA((6,)),
            pltpu.SemaphoreType.DMA((5,)),
        ],
        compiler_params=pltpu.CompilerParams(vmem_limit_bytes=40 << 20),
        cost_estimate=pl.CostEstimate(flops=1000, transcendentals=0, bytes_accessed=1000),
        name="encoder_forward",
    )(flag, frame, ln_gain, in_hbm(w_qkv))


def encoder_backward_kernel(
    flag_ref,
    grad_ref,
    gain_ref,
    qkv_ref,
    probs_ref,
    norm_ref,
    inv_ref,
    w_hbm,
    out_ref,
    w_buf,
    work,
    mix,
    sems,
):
    @pl.when(flag_ref[0] == 0)
    def _():
        out_ref[...] = jnp.zeros_like(out_ref)

    @pl.when(flag_ref[0] == 1)
    def _():
        f32, bf16 = jnp.float32, jnp.bfloat16
        copies = weight_copies(w_hbm, w_buf, sems)
        for copy in copies:
            copy.start()
        vis = w_hbm.shape[0]
        tokens = grad_ref.shape[1]
        gain = gain_ref[...].astype(f32)
        order = token_order(4 * tokens)
        for half in range(2):
            grads = jnp.concatenate([grad_ref[j * 2 + half] for j in range(4)], axis=0)
            work[half] = dot(order, grads, TN) * gain[:, half * CHUNK : (half + 1) * CHUNK]
        mean = (
            jnp.sum(work[0], axis=1, keepdims=True) + jnp.sum(work[1], axis=1, keepdims=True)
        ) / vis
        along = (
            jnp.sum(work[0] * norm_ref[0], axis=1, keepdims=True)
            + jnp.sum(work[1] * norm_ref[1], axis=1, keepdims=True)
        ) / vis
        inverse = inv_ref[...]
        for half in range(2):
            work[half] = inverse * (work[half] - mean - norm_ref[half] * along)
        total = jnp.zeros((work.shape[1], vis), f32)
        for half in range(2):
            mixed = [{}, {}, {}]
            for head in range(CHUNK_HEADS):
                start, stop, low, high = head_window(head)
                grad = head_only(work[half, :, start:stop].astype(bf16), low, high)
                query = head_only(qkv_ref[half * 3, :, start:stop], low, high)
                key = head_only(qkv_ref[half * 3 + 1, :, start:stop], low, high)
                value = qkv_ref[half * 3 + 2, :, start:stop]
                probs = probs_ref[half * CHUNK_HEADS + head]
                grad_weights = dot(grad, value, NT)
                inner = jnp.sum(grad_weights * probs, axis=1, keepdims=True)
                scores = (probs * (grad_weights - inner) * HDIM ** (-0.5)).astype(bf16)
                add_tiles(mixed[2], dot(probs.astype(bf16), grad, TN), start)
                add_tiles(mixed[0], dot(scores, key, NN), start)
                add_tiles(mixed[1], dot(scores, query, TN), start)
            for kind in range(3):
                for tile, part in mixed[kind].items():
                    mix[kind, :, tile * 128 : (tile + 1) * 128] = part.astype(bf16)
            for kind in range(3):
                i = half * 3 + kind
                copies[i].wait()
                total = total + dot(mix[kind], w_buf[i], NT)
        for half in range(2):
            columns = slice(half * CHUNK, (half + 1) * CHUNK)
            out_ref[:, columns] = (work[half] + total[:, columns]).astype(bf16)


def encoder_backward(flag, w_qkv, ln_gain, qkv, probs, norm, inverse, grad):
    length, vis = norm.shape[1], w_qkv.shape[0]
    bf16, f32 = jnp.bfloat16, jnp.float32
    vmem = pl.BlockSpec(memory_space=pltpu.VMEM)
    return pl.pallas_call(
        encoder_backward_kernel,
        out_shape=jax.ShapeDtypeStruct((length, vis), bf16),
        in_specs=[pl.BlockSpec(memory_space=pltpu.SMEM)]
        + [vmem] * 6
        + [pl.BlockSpec(memory_space=pltpu.HBM)],
        out_specs=vmem,
        scratch_shapes=[
            pltpu.VMEM((6, vis, CHUNK), bf16),
            pltpu.VMEM((2, length, CHUNK), f32),
            pltpu.VMEM((3, length, CHUNK), bf16),
            pltpu.SemaphoreType.DMA((6,)),
        ],
        compiler_params=pltpu.CompilerParams(vmem_limit_bytes=40 << 20),
        cost_estimate=pl.CostEstimate(flops=1000, transcendentals=0, bytes_accessed=1000),
        name="encoder_backward",
    )(flag, grad, ln_gain, qkv, probs, norm, inverse, in_hbm(w_qkv))


def give_columns_kernel(start, flag_ref, after_ref, w_hbm, out_ref, sem):
    @pl.when(flag_ref[0] == 0)
    def _():
        copy = pltpu.make_async_copy(w_hbm.at[:, pl.ds(start, out_ref.shape[1])], out_ref, sem)
        copy.start()
        copy.wait()


def give_columns(flag, after, matrix, start, size):
    return pl.pallas_call(
        lambda *refs: give_columns_kernel(start, *refs),
        out_shape=jax.ShapeDtypeStruct((matrix.shape[0], size), matrix.dtype),
        in_specs=[
            pl.BlockSpec(memory_space=pltpu.SMEM),
            pl.BlockSpec(memory_space=pl.ANY),
            pl.BlockSpec(memory_space=pltpu.HBM),
        ],
        out_specs=pl.BlockSpec(memory_space=pltpu.VMEM),
        scratch_shapes=[pltpu.SemaphoreType.DMA],
        compiler_params=pltpu.CompilerParams(vmem_limit_bytes=16 << 20),
        cost_estimate=pl.CostEstimate(flops=1000, transcendentals=0, bytes_accessed=1000),
        name="give_columns",
    )(flag, after, in_hbm(matrix))


def give_cotangent_kernel(flag_ref, after_ref, gain_ref, cot_hbm, out_ref, sem):
    @pl.when(flag_ref[0] == 0)
    def _():
        rows, size = cot_hbm.shape[0], out_ref.shape[1]
        copy = pltpu.make_async_copy(
            cot_hbm.at[:, pl.ds(0, size)], out_ref.at[pl.ds(0, rows)], sem
        )
        copy.start()
        out_ref[rows:] = jnp.broadcast_to(gain_ref[:, :size], (GAIN_ROWS, size))
        copy.wait()


def give_cotangent(flag, after, gain, cot, size):
    return pl.pallas_call(
        give_cotangent_kernel,
        out_shape=jax.ShapeDtypeStruct((cot.shape[0] + GAIN_ROWS, size), cot.dtype),
        in_specs=[
            pl.BlockSpec(memory_space=pltpu.SMEM),
            pl.BlockSpec(memory_space=pl.ANY),
            pl.BlockSpec(memory_space=pltpu.VMEM),
            pl.BlockSpec(memory_space=pltpu.HBM),
        ],
        out_specs=pl.BlockSpec(memory_space=pltpu.VMEM),
        scratch_shapes=[pltpu.SemaphoreType.DMA],
        compiler_params=pltpu.CompilerParams(vmem_limit_bytes=16 << 20),
        cost_estimate=pl.CostEstimate(flops=1000, transcendentals=0, bytes_accessed=1000),
        name="give_cotangent",
    )(flag, after, gain, in_hbm(cot))


def in_hbm(array):
    return pltpu.with_memory_space_constraint(array, pltpu.HBM)


def partial_kernel(start, flag_ref, x_ref, got_ref, mine_ref, near_ref, late_ref, *refs):
    *homes, w_ref, sem = refs
    size = w_ref.shape[1]

    @pl.when(flag_ref[0] == 1)
    def _():
        copy = pltpu.make_async_copy(got_ref, w_ref, sem)
        copy.start()
        copy.wait()

    @pl.when(flag_ref[0] == 0)
    def _():
        copy = pltpu.make_async_copy(mine_ref.at[:, pl.ds(start, size)], w_ref, sem)
        copy.start()
        copy.wait()

    pairs, _, rows, depth = x_ref.shape
    weight = w_ref[...]
    away = dot(x_ref[:, 1].reshape(pairs * rows, depth), weight, NN)
    away = [away[s * rows : (s + 1) * rows].astype(near_ref.dtype) for s in range(pairs)]
    for i, s in enumerate(near_blocks(pairs)):
        near_ref[i] = away[s]
    for i, s in enumerate(late_blocks(pairs)):
        late_ref[i] = away[s]
    home = dot(x_ref[:, 0].reshape(pairs * rows, depth), weight, NN)
    for s in range(pairs):
        homes[s][...] = home[s * rows : (s + 1) * rows]


def near_blocks(pairs):
    return list(range(1, pairs // 2 + 1))


def late_blocks(pairs):
    return list(range(pairs // 2 + 1, pairs)) + [0]


def partial_products(flag, features, got, matrix, start):
    pairs, _, rows, depth = features.shape
    size = got.shape[1]
    vmem = pl.BlockSpec(memory_space=pltpu.VMEM)
    half = jax.ShapeDtypeStruct((pairs // 2, rows, size), jnp.bfloat16)
    near, late, *home, weight = pl.pallas_call(
        lambda *refs: partial_kernel(start, *refs),
        out_shape=(half, half)
        + (jax.ShapeDtypeStruct((rows, size), jnp.float32),) * pairs
        + (jax.ShapeDtypeStruct((depth, size), got.dtype),),
        in_specs=[
            pl.BlockSpec(memory_space=pltpu.SMEM),
            vmem,
            pl.BlockSpec(memory_space=pl.ANY),
            pl.BlockSpec(memory_space=pltpu.HBM),
        ],
        out_specs=(vmem,) * (3 + pairs),
        scratch_shapes=[pltpu.SemaphoreType.DMA],
        compiler_params=pltpu.CompilerParams(vmem_limit_bytes=32 << 20),
        cost_estimate=pl.CostEstimate(flops=1000, transcendentals=0, bytes_accessed=1000),
        name="partial_products",
    )(flag, features, in_hbm(got), in_hbm(matrix))
    return near, late, home, weight


def arrange_in_kernel(flag_ref, order_ref, a_ref, b_ref, out_ref):
    keep = flag_ref[0] == 1
    for r in range(out_ref.shape[0]):
        place = order_ref[r]
        out_ref[r] = jnp.where(keep, a_ref[place], b_ref[place])


def arrange_last_kernel(order_ref, near_ref, far_ref, out_ref):
    for s in range(near_ref.shape[0]):
        out_ref[order_ref[2 * s]] = near_ref[s]
        out_ref[order_ref[2 * s + 1]] = far_ref[s]


def arrange(kernel, name, scalars, a, b):
    vmem = pl.BlockSpec(memory_space=pltpu.VMEM)
    return pl.pallas_call(
        kernel,
        out_shape=jax.ShapeDtypeStruct((scalars[-1].shape[0],) + b.shape[1:], b.dtype),
        in_specs=[pl.BlockSpec(memory_space=pltpu.SMEM)] * len(scalars) + [vmem, vmem],
        out_specs=vmem,
        compiler_params=pltpu.CompilerParams(vmem_limit_bytes=32 << 20),
        name=name,
    )(*scalars, a, b)


def passed_along(block, axis, distance):
    devices = range(lax.axis_size(axis))
    route = [(i - distance, i) for i in devices if i - distance in devices]
    return lax.ppermute(block, axis, route)


def rotated(blocks, shift):
    count = blocks.shape[0]
    step = 1
    while step < count:
        turned = jnp.concatenate([blocks[step:], blocks[:step]], axis=0)
        blocks = jnp.where((shift // step) % 2 == 1, turned, blocks)
        step *= 2
    return blocks


def sent_round(block, move):
    count = lax.axis_size("dp")
    return lax.ppermute(block, "dp", [(i, i ^ (2 * move)) for i in range(count)])


def sent_across(block):
    return lax.ppermute(block, "dp", [(i, i ^ 1) for i in range(lax.axis_size("dp"))])


def sent_tp(block, distance):
    count = lax.axis_size("tp")
    return lax.ppermute(block, "tp", [(i, (i + distance) % count) for i in range(count)])


def per_device(frames, counts, w_qkv, ln_gain, w_proj, rms_gain, cotangent):
    f32, bf16 = jnp.float32, jnp.bfloat16
    is_encoder = lax.axis_index("grp") == 0
    flag = is_encoder.astype(jnp.int32).reshape(1)
    dp_count, tp_count = lax.axis_size("dp"), lax.axis_size("tp")
    pair_count = dp_count // 2
    dp_index, tp_index = lax.axis_index("dp"), lax.axis_index("tp")
    relative = jnp.arange(dp_count, dtype=jnp.int32)
    order = dp_index ^ relative

    frame = frames[0, 0]
    tokens_here = frame.shape[0] // 4
    depth = w_proj.shape[1]
    half = w_proj.shape[2] // 2
    first = half * FIRST_PART // 16 // 128 * 128
    sizes = (first, half - first)

    w_mine, cot_mine = w_proj[0], cotangent[0]
    give = [give_columns(flag, flag, w_mine, 0, sizes[0])]
    give.append(give_columns(flag, give[0], w_mine, first, sizes[1]))
    got = [passed_along(block, "grp", -1) for block in give]
    give_cot = give_cotangent(flag, give[1], rms_gain, cot_mine, half)

    embedded, qkv, probs, norm, inverse = encoder_forward(flag, frame, w_qkv[0], ln_gain)

    pieces = embedded
    if depth != CHUNK:
        pieces = embedded.reshape(-1, tokens_here, CHUNK // depth, depth)
        pieces = pieces.transpose(0, 2, 1, 3).reshape(dp_count, tokens_here, depth)
    swapped = lax.all_to_all(pieces, "dp", 0, 0)
    arrived = passed_along(swapped, "grp", 1)
    swapped, give_cot = lax.optimization_barrier((swapped, give_cot))
    got_cot = passed_along(give_cot, "grp", -1)
    features = arrange(arrange_in_kernel, "arrange_in", (flag, order), swapped, arrived)
    features = jnp.concatenate(
        [features] + [sent_tp(features, tp_count - s) for s in range(1, tp_count)], axis=1
    ).reshape(pair_count, 2, tp_count * tokens_here, depth)

    acts, weights = [], []
    for c in range(2):
        near, late, home, weight = partial_products(flag, features, got[c], w_mine, half + c * first)
        weights.append(weight)
        near, late = sent_across(near), sent_across(late)
        for i, s in enumerate(near_blocks(pair_count)):
            home[s] = home[s] + near[i].astype(f32)
        for i, s in enumerate(late_blocks(pair_count)):
            home[s] = home[s] + late[i].astype(f32)
        sends = [block.astype(bf16) for block in home[1:]]
        if c == 0:
            sends, features = lax.optimization_barrier((sends, features))
        total = home[0]
        for s, block in enumerate(sends):
            total = total + sent_round(block, s + 1).astype(f32)
        acts.append(total)

    got_cot, acts[0] = lax.optimization_barrier((got_cot, acts[0]))
    rows = cot_mine.shape[0]
    cot = jnp.where(is_encoder, got_cot[:rows], cot_mine[:, half:])
    gain_rms = jnp.where(is_encoder, got_cot[rows : rows + 1], rms_gain[:, half:])
    slot = lax.broadcasted_iota(jnp.int32, (1, tokens_here), 1) // TOKF
    live_mask = (slot < rotated(counts, tp_index)[:, None]).astype(f32).reshape(-1, 1)
    cot = rotated(cot.reshape(tp_count, tokens_here, half), tp_index).reshape(-1, half)
    scaled = gain_rms.astype(f32) * cot.astype(f32) * live_mask
    scaled = (scaled[:, :first], scaled[:, first:])
    squares = sum(jnp.sum(act * act, axis=1) for act in acts)
    products = sum(jnp.sum(act * part, axis=1) for act, part in zip(acts, scaled))
    sums = jnp.stack([squares, products], axis=1).reshape(tp_count, tokens_here, 2)
    sums = lax.psum(rotated(sums, (tp_count - tp_index) % tp_count), ("grp", "tp"))
    sums = rotated(sums, tp_index).reshape(-1, 2)
    inverse_rms = lax.rsqrt(sums[:, :1] / D + 1e-06)
    fall = inverse_rms**3 * (sums[:, 1:] / D)
    grads = [
        (inverse_rms * part - act * fall).astype(bf16) for act, part in zip(acts, scaled)
    ]

    def gathered_round(block):
        blocks = [block] + [None] * (pair_count - 1)
        for s in range(1, pair_count):
            blocks[s] = sent_round(block, s)
        return jnp.stack(blocks)

    near = gathered_round(grads[0])
    duo = jnp.stack([grads[1], sent_across(grads[1])])
    near, duo = lax.optimization_barrier((near, duo))
    far = sent_across(near)
    duos = gathered_round(duo)
    near, far = (near, duos[:, 0]), (far, duos[:, 1])

    def back(blocks):
        return sum(
            jnp.einsum("prc,kc->prk", block, weight, preferred_element_type=f32)
            for block, weight in zip(blocks, weights)
        )

    terms = [back(near), back(far)]
    terms = jnp.stack(
        [term.reshape(pair_count, tp_count, tokens_here, depth) for term in terms], axis=1
    ).reshape(dp_count, tp_count, tokens_here, depth)
    total = terms[:, 0]
    for s in range(1, tp_count):
        total = total + sent_tp(terms[:, s].astype(bf16), s).astype(f32)
    total = total.astype(bf16)
    total = total.reshape(pair_count, 2, tokens_here, depth)
    middle = pair_count // 2
    summed = [None] * pair_count
    for start, stop in ((middle, pair_count), (0, middle)):
        part = total[start:stop]
        part = part.astype(f32) + passed_along(part, "grp", -1).astype(f32)
        for s in range(start, stop):
            summed[s] = part[s - start].astype(bf16)
    blocks = [summed[0]] + [sent_round(summed[s], s) for s in range(1, pair_count)]
    near = jnp.stack([block[0] for block in blocks])
    far = sent_across(jnp.stack([block[1] for block in blocks]))
    whole = arrange(arrange_last_kernel, "arrange_last", (order,), near, far)
    if depth != CHUNK:
        whole = whole.reshape(-1, CHUNK // depth, tokens_here, depth)
        whole = whole.transpose(0, 2, 1, 3).reshape(-1, tokens_here, CHUNK)

    grad_frames = encoder_backward(flag, w_qkv[0], ln_gain, qkv, probs, norm, inverse, whole)
    return grad_frames[None, None]


def solution(mesh):
    placed = (
        P("grp", ("dp", "tp"), None, None),
        P("dp"),
        P("grp", None, None),
        P("grp", None),
        P("grp", "dp", "tp"),
        P("grp", "tp"),
        P("grp", "dp", "tp"),
    )
    return jax.shard_map(
        per_device,
        mesh=mesh,
        in_specs=placed,
        out_specs=P("grp", ("dp", "tp"), None, None),
        check_vma=False,
    )
```

```python
import jax
import jax.numpy as jnp
from jax import lax
from jax.experimental import pallas as pl
from jax.experimental.pallas import tpu as pltpu
from jax.sharding import PartitionSpec as P

HEADS = 16
HDIM = 80
D = 8192
TOKF = 32
FIRST_PART = 9
GAIN_ROWS = 16
CHUNK = 640
CHUNK_HEADS = CHUNK // HDIM


def head_window(head):
    low, high = head * HDIM, (head + 1) * HDIM
    start, stop = low // 128 * 128, -(-high // 128) * 128
    return start, stop, low - start, high - start


def head_only(block, low, high):
    lane = lax.broadcasted_iota(jnp.int32, block.shape, 1)
    return jnp.where((lane >= low) & (lane < high), block, jnp.zeros_like(block))


def dot(a, b, dims):
    return lax.dot_general(a, b, (dims, ((), ())), preferred_element_type=jnp.float32)


def add_tiles(tiles, block, start):
    for i in range(block.shape[1] // 128):
        tile = start // 128 + i
        part = block[:, i * 128 : (i + 1) * 128]
        tiles[tile] = part if tile not in tiles else tiles[tile] + part


NT = ((1,), (1,))
NN = ((1,), (0,))
TN = ((0,), (0,))


def token_order(length):
    row = lax.broadcasted_iota(jnp.int32, (length, length), 0)
    column = lax.broadcasted_iota(jnp.int32, (length, length), 1)
    tokens = length // 4
    return (row % tokens * 4 + row // tokens == column).astype(jnp.bfloat16)


def weight_copies(w_hbm, w_buf, sems):
    return [
        pltpu.make_async_copy(
            w_hbm.at[:, pl.ds(((i % 3) * 2 + i // 3) * CHUNK, CHUNK)], w_buf.at[i], sems.at[i]
        )
        for i in range(6)
    ]


def encoder_forward_kernel(
    flag_ref,
    x_ref,
    gain_ref,
    w_hbm,
    emb_ref,
    qkv_hbm,
    probs_hbm,
    norm_hbm,
    inv_ref,
    w_buf,
    qkv_ref,
    probs_ref,
    norm_ref,
    work,
    sems,
    out_sems,
):
    @pl.when(flag_ref[0] == 1)
    def _():
        copies = weight_copies(w_hbm, w_buf, sems)
        for copy in copies:
            copy.start()
        outs = []
        x = x_ref[...]
        vis = x.shape[1]
        for half in range(2):
            for kind in range(3):
                i = half * 3 + kind
                copies[i].wait()
                qkv_ref[i] = dot(x, w_buf[i], NN).astype(jnp.bfloat16)
            heads = pl.ds(half * CHUNK_HEADS, CHUNK_HEADS)
            outs.append(
                pltpu.make_async_copy(
                    qkv_ref.at[pl.ds(half * 3, 3)],
                    qkv_hbm.at[pl.ds(half * 3, 3)],
                    out_sems.at[half],
                )
            )
            outs[-1].start()
            tiles = {}
            add_tiles(tiles, x[:, half * CHUNK : (half + 1) * CHUNK].astype(jnp.float32), 0)
            for head in range(CHUNK_HEADS):
                start, stop, low, high = head_window(head)
                query = qkv_ref[half * 3, :, start:stop]
                key = head_only(qkv_ref[half * 3 + 1, :, start:stop], low, high)
                value = head_only(qkv_ref[half * 3 + 2, :, start:stop], low, high)
                scores = dot(query, key, NT) * HDIM ** (-0.5)
                weights = jnp.exp(scores - jnp.max(scores, axis=1, keepdims=True))
                weights = weights / jnp.sum(weights, axis=1, keepdims=True)
                probs_ref[half * CHUNK_HEADS + head] = weights
                add_tiles(tiles, dot(weights.astype(jnp.bfloat16), value, NN), start)
            for tile, part in tiles.items():
                work[half, :, tile * 128 : (tile + 1) * 128] = part
            outs.append(
                pltpu.make_async_copy(probs_ref.at[heads], probs_hbm.at[heads], out_sems.at[2 + half])
            )
            outs[-1].start()
        first, second = work[0], work[1]
        mean = (
            jnp.sum(first, axis=1, keepdims=True) + jnp.sum(second, axis=1, keepdims=True)
        ) / vis
        first, second = first - mean, second - mean
        variance = (
            jnp.sum(first * first, axis=1, keepdims=True)
            + jnp.sum(second * second, axis=1, keepdims=True)
        ) / vis
        inverse = lax.rsqrt(variance + 1e-06)
        inv_ref[...] = inverse
        gain = gain_ref[...].astype(jnp.float32)
        tokens = x.shape[0] // 4
        order = token_order(x.shape[0])
        for half, centred in enumerate((first, second)):
            normal = centred * inverse
            norm_ref[half] = normal
            embedded = (normal * gain[:, half * CHUNK : (half + 1) * CHUNK]).astype(jnp.bfloat16)
            embedded = dot(order, embedded, NN).astype(jnp.bfloat16)
            for j in range(4):
                emb_ref[j * 2 + half] = embedded[j * tokens : (j + 1) * tokens]
        outs.append(pltpu.make_async_copy(norm_ref, norm_hbm, out_sems.at[4]))
        outs[-1].start()
        for copy in outs:
            copy.wait()


def encoder_forward(flag, frame, w_qkv, ln_gain):
    length, vis = frame.shape
    bf16, f32 = jnp.bfloat16, jnp.float32
    vmem = pl.BlockSpec(memory_space=pltpu.VMEM)
    hbm = pl.BlockSpec(memory_space=pltpu.HBM)
    return pl.pallas_call(
        encoder_forward_kernel,
        out_shape=(
            jax.ShapeDtypeStruct((8, length // 4, CHUNK), bf16),
            pltpu.HBM((6, length, CHUNK), bf16),
            pltpu.HBM((HEADS, length, length), f32),
            pltpu.HBM((2, length, CHUNK), f32),
            jax.ShapeDtypeStruct((length, 1), f32),
        ),
        in_specs=[pl.BlockSpec(memory_space=pltpu.SMEM), vmem, vmem, hbm],
        out_specs=(vmem, hbm, hbm, hbm, vmem),
        scratch_shapes=[
            pltpu.VMEM((6, vis, CHUNK), bf16),
            pltpu.VMEM((6, length, CHUNK), bf16),
            pltpu.VMEM((HEADS, length, length), f32),
            pltpu.VMEM((2, length, CHUNK), f32),
            pltpu.VMEM((2, length, CHUNK), f32),
            pltpu.SemaphoreType.DMA((6,)),
            pltpu.SemaphoreType.DMA((5,)),
        ],
        compiler_params=pltpu.CompilerParams(vmem_limit_bytes=24 << 20),
        cost_estimate=pl.CostEstimate(flops=1000, transcendentals=0, bytes_accessed=1000),
        name="encoder_forward",
    )(flag, frame, ln_gain, in_hbm(w_qkv))


def encoder_backward_kernel(
    flag_ref,
    grad_ref,
    gain_ref,
    qkv_ref,
    probs_ref,
    norm_ref,
    inv_ref,
    w_hbm,
    out_ref,
    w_buf,
    work,
    mix,
    sems,
):
    @pl.when(flag_ref[0] == 0)
    def _():
        out_ref[...] = jnp.zeros_like(out_ref)

    @pl.when(flag_ref[0] == 1)
    def _():
        f32, bf16 = jnp.float32, jnp.bfloat16
        copies = weight_copies(w_hbm, w_buf, sems)
        for copy in copies:
            copy.start()
        vis = w_hbm.shape[0]
        tokens = grad_ref.shape[1]
        gain = gain_ref[...].astype(f32)
        order = token_order(4 * tokens)
        for half in range(2):
            grads = jnp.concatenate([grad_ref[j * 2 + half] for j in range(4)], axis=0)
            work[half] = dot(order, grads, TN) * gain[:, half * CHUNK : (half + 1) * CHUNK]
        mean = (
            jnp.sum(work[0], axis=1, keepdims=True) + jnp.sum(work[1], axis=1, keepdims=True)
        ) / vis
        along = (
            jnp.sum(work[0] * norm_ref[0], axis=1, keepdims=True)
            + jnp.sum(work[1] * norm_ref[1], axis=1, keepdims=True)
        ) / vis
        inverse = inv_ref[...]
        for half in range(2):
            work[half] = inverse * (work[half] - mean - norm_ref[half] * along)
        total = jnp.zeros((work.shape[1], vis), f32)
        for half in range(2):
            mixed = [{}, {}, {}]
            for head in range(CHUNK_HEADS):
                start, stop, low, high = head_window(head)
                grad = head_only(work[half, :, start:stop].astype(bf16), low, high)
                query = head_only(qkv_ref[half * 3, :, start:stop], low, high)
                key = head_only(qkv_ref[half * 3 + 1, :, start:stop], low, high)
                value = qkv_ref[half * 3 + 2, :, start:stop]
                probs = probs_ref[half * CHUNK_HEADS + head]
                grad_weights = dot(grad, value, NT)
                inner = jnp.sum(grad_weights * probs, axis=1, keepdims=True)
                scores = (probs * (grad_weights - inner) * HDIM ** (-0.5)).astype(bf16)
                add_tiles(mixed[2], dot(probs.astype(bf16), grad, TN), start)
                add_tiles(mixed[0], dot(scores, key, NN), start)
                add_tiles(mixed[1], dot(scores, query, TN), start)
            for kind in range(3):
                for tile, part in mixed[kind].items():
                    mix[kind, :, tile * 128 : (tile + 1) * 128] = part.astype(bf16)
            for kind in range(3):
                i = half * 3 + kind
                copies[i].wait()
                total = total + dot(mix[kind], w_buf[i], NT)
        for half in range(2):
            columns = slice(half * CHUNK, (half + 1) * CHUNK)
            out_ref[:, columns] = (work[half] + total[:, columns]).astype(bf16)


def encoder_backward(flag, w_qkv, ln_gain, qkv, probs, norm, inverse, grad):
    length, vis = norm.shape[1], w_qkv.shape[0]
    bf16, f32 = jnp.bfloat16, jnp.float32
    vmem = pl.BlockSpec(memory_space=pltpu.VMEM)
    return pl.pallas_call(
        encoder_backward_kernel,
        out_shape=jax.ShapeDtypeStruct((length, vis), bf16),
        in_specs=[pl.BlockSpec(memory_space=pltpu.SMEM)]
        + [vmem] * 6
        + [pl.BlockSpec(memory_space=pltpu.HBM)],
        out_specs=vmem,
        scratch_shapes=[
            pltpu.VMEM((6, vis, CHUNK), bf16),
            pltpu.VMEM((2, length, CHUNK), f32),
            pltpu.VMEM((3, length, CHUNK), bf16),
            pltpu.SemaphoreType.DMA((6,)),
        ],
        compiler_params=pltpu.CompilerParams(vmem_limit_bytes=26 << 20),
        cost_estimate=pl.CostEstimate(flops=1000, transcendentals=0, bytes_accessed=1000),
        name="encoder_backward",
    )(flag, grad, ln_gain, qkv, probs, norm, inverse, in_hbm(w_qkv))


def give_columns_kernel(start, flag_ref, after_ref, w_hbm, out_ref, sem):
    @pl.when(flag_ref[0] == 0)
    def _():
        copy = pltpu.make_async_copy(w_hbm.at[:, pl.ds(start, out_ref.shape[1])], out_ref, sem)
        copy.start()
        copy.wait()


def give_columns(flag, after, matrix, start, size):
    return pl.pallas_call(
        lambda *refs: give_columns_kernel(start, *refs),
        out_shape=jax.ShapeDtypeStruct((matrix.shape[0], size), matrix.dtype),
        in_specs=[
            pl.BlockSpec(memory_space=pltpu.SMEM),
            pl.BlockSpec(memory_space=pl.ANY),
            pl.BlockSpec(memory_space=pltpu.HBM),
        ],
        out_specs=pl.BlockSpec(memory_space=pltpu.VMEM),
        scratch_shapes=[pltpu.SemaphoreType.DMA],
        compiler_params=pltpu.CompilerParams(vmem_limit_bytes=16 << 20),
        cost_estimate=pl.CostEstimate(flops=1000, transcendentals=0, bytes_accessed=1000),
        name="give_columns",
    )(flag, after, in_hbm(matrix))


def give_cotangent_kernel(flag_ref, after_ref, gain_ref, cot_hbm, out_ref, sem):
    @pl.when(flag_ref[0] == 0)
    def _():
        rows, size = cot_hbm.shape[0], out_ref.shape[1]
        copy = pltpu.make_async_copy(
            cot_hbm.at[:, pl.ds(0, size)], out_ref.at[pl.ds(0, rows)], sem
        )
        copy.start()
        out_ref[rows:] = jnp.broadcast_to(gain_ref[:, :size], (GAIN_ROWS, size))
        copy.wait()


def give_cotangent(flag, after, gain, cot, size):
    return pl.pallas_call(
        give_cotangent_kernel,
        out_shape=jax.ShapeDtypeStruct((cot.shape[0] + GAIN_ROWS, size), cot.dtype),
        in_specs=[
            pl.BlockSpec(memory_space=pltpu.SMEM),
            pl.BlockSpec(memory_space=pl.ANY),
            pl.BlockSpec(memory_space=pltpu.VMEM),
            pl.BlockSpec(memory_space=pltpu.HBM),
        ],
        out_specs=pl.BlockSpec(memory_space=pltpu.VMEM),
        scratch_shapes=[pltpu.SemaphoreType.DMA],
        compiler_params=pltpu.CompilerParams(vmem_limit_bytes=16 << 20),
        cost_estimate=pl.CostEstimate(flops=1000, transcendentals=0, bytes_accessed=1000),
        name="give_cotangent",
    )(flag, after, gain, in_hbm(cot))


def in_hbm(array):
    return pltpu.with_memory_space_constraint(array, pltpu.HBM)


def partial_kernel(start, flag_ref, x_ref, got_ref, mine_ref, near_ref, late_ref, *refs):
    *homes, w_ref, sem = refs
    size = w_ref.shape[1]

    @pl.when(flag_ref[0] == 1)
    def _():
        copy = pltpu.make_async_copy(got_ref, w_ref, sem)
        copy.start()
        copy.wait()

    @pl.when(flag_ref[0] == 0)
    def _():
        copy = pltpu.make_async_copy(mine_ref.at[:, pl.ds(start, size)], w_ref, sem)
        copy.start()
        copy.wait()

    pairs, _, rows, depth = x_ref.shape
    weight = w_ref[...]
    away = dot(x_ref[:, 1].reshape(pairs * rows, depth), weight, NN)
    away = [away[s * rows : (s + 1) * rows].astype(near_ref.dtype) for s in range(pairs)]
    for i, s in enumerate(near_blocks(pairs)):
        near_ref[i] = away[s]
    for i, s in enumerate(late_blocks(pairs)):
        late_ref[i] = away[s]
    home = dot(x_ref[:, 0].reshape(pairs * rows, depth), weight, NN)
    for s in range(pairs):
        homes[s][...] = home[s * rows : (s + 1) * rows]


def near_blocks(pairs):
    return list(range(1, pairs // 2 + 1))


def late_blocks(pairs):
    return list(range(pairs // 2 + 1, pairs)) + [0]


def partial_products(flag, features, got, matrix, start):
    pairs, _, rows, depth = features.shape
    size = got.shape[1]
    vmem = pl.BlockSpec(memory_space=pltpu.VMEM)
    half = jax.ShapeDtypeStruct((pairs // 2, rows, size), jnp.bfloat16)
    near, late, *home, weight = pl.pallas_call(
        lambda *refs: partial_kernel(start, *refs),
        out_shape=(half, half)
        + (jax.ShapeDtypeStruct((rows, size), jnp.float32),) * pairs
        + (jax.ShapeDtypeStruct((depth, size), got.dtype),),
        in_specs=[
            pl.BlockSpec(memory_space=pltpu.SMEM),
            vmem,
            pl.BlockSpec(memory_space=pl.ANY),
            pl.BlockSpec(memory_space=pltpu.HBM),
        ],
        out_specs=(vmem,) * (3 + pairs),
        scratch_shapes=[pltpu.SemaphoreType.DMA],
        compiler_params=pltpu.CompilerParams(vmem_limit_bytes=20 << 20),
        cost_estimate=pl.CostEstimate(flops=1000, transcendentals=0, bytes_accessed=1000),
        name="partial_products",
    )(flag, features, in_hbm(got), in_hbm(matrix))
    return near, late, home, weight


def arrange_in_kernel(flag_ref, order_ref, a_ref, b_ref, out_ref):
    keep = flag_ref[0] == 1
    for r in range(out_ref.shape[0]):
        place = order_ref[r]
        out_ref[r] = jnp.where(keep, a_ref[place], b_ref[place])


def arrange_last_kernel(order_ref, near_ref, far_ref, out_ref):
    for s in range(near_ref.shape[0]):
        out_ref[order_ref[2 * s]] = near_ref[s]
        out_ref[order_ref[2 * s + 1]] = far_ref[s]


def arrange(kernel, name, scalars, a, b):
    vmem = pl.BlockSpec(memory_space=pltpu.VMEM)
    return pl.pallas_call(
        kernel,
        out_shape=jax.ShapeDtypeStruct((scalars[-1].shape[0],) + b.shape[1:], b.dtype),
        in_specs=[pl.BlockSpec(memory_space=pltpu.SMEM)] * len(scalars) + [vmem, vmem],
        out_specs=vmem,
        compiler_params=pltpu.CompilerParams(vmem_limit_bytes=32 << 20),
        name=name,
    )(*scalars, a, b)


def passed_along(block, axis, distance):
    devices = range(lax.axis_size(axis))
    route = [(i - distance, i) for i in devices if i - distance in devices]
    return lax.ppermute(block, axis, route)


def rotated(blocks, shift):
    count = blocks.shape[0]
    step = 1
    while step < count:
        turned = jnp.concatenate([blocks[step:], blocks[:step]], axis=0)
        blocks = jnp.where((shift // step) % 2 == 1, turned, blocks)
        step *= 2
    return blocks


def sent_round(block, move):
    count = lax.axis_size("dp")
    return lax.ppermute(block, "dp", [(i, i ^ (2 * move)) for i in range(count)])


def sent_across(block):
    return lax.ppermute(block, "dp", [(i, i ^ 1) for i in range(lax.axis_size("dp"))])


def sent_tp(block, distance):
    count = lax.axis_size("tp")
    return lax.ppermute(block, "tp", [(i, (i + distance) % count) for i in range(count)])


def per_device(frames, counts, w_qkv, ln_gain, w_proj, rms_gain, cotangent):
    f32, bf16 = jnp.float32, jnp.bfloat16
    is_encoder = lax.axis_index("grp") == 0
    flag = is_encoder.astype(jnp.int32).reshape(1)
    dp_count, tp_count = lax.axis_size("dp"), lax.axis_size("tp")
    pair_count = dp_count // 2
    dp_index, tp_index = lax.axis_index("dp"), lax.axis_index("tp")
    relative = jnp.arange(dp_count, dtype=jnp.int32)
    order = dp_index ^ relative

    frame = frames[0, 0]
    tokens_here = frame.shape[0] // 4
    depth = w_proj.shape[1]
    half = w_proj.shape[2] // 2
    first = half * FIRST_PART // 16 // 128 * 128
    sizes = (first, half - first)

    w_mine, cot_mine = w_proj[0], cotangent[0]
    give = [give_columns(flag, flag, w_mine, 0, sizes[0])]
    give.append(give_columns(flag, give[0], w_mine, first, sizes[1]))
    got = [passed_along(block, "grp", -1) for block in give]
    give_cot = give_cotangent(flag, give[1], rms_gain, cot_mine, half)

    embedded, qkv, probs, norm, inverse = encoder_forward(flag, frame, w_qkv[0], ln_gain)

    pieces = embedded
    if depth != CHUNK:
        pieces = embedded.reshape(-1, tokens_here, CHUNK // depth, depth)
        pieces = pieces.transpose(0, 2, 1, 3).reshape(dp_count, tokens_here, depth)
    swapped = lax.all_to_all(pieces, "dp", 0, 0)
    arrived = passed_along(swapped, "grp", 1)
    swapped, give_cot = lax.optimization_barrier((swapped, give_cot))
    got_cot = passed_along(give_cot, "grp", -1)
    features = arrange(arrange_in_kernel, "arrange_in", (flag, order), swapped, arrived)
    features = jnp.concatenate(
        [features] + [sent_tp(features, tp_count - s) for s in range(1, tp_count)], axis=1
    ).reshape(pair_count, 2, tp_count * tokens_here, depth)

    acts, weights = [], []
    for c in range(2):
        near, late, home, weight = partial_products(flag, features, got[c], w_mine, half + c * first)
        weights.append(weight)
        near, late = sent_across(near), sent_across(late)
        for i, s in enumerate(near_blocks(pair_count)):
            home[s] = home[s] + near[i].astype(f32)
        for i, s in enumerate(late_blocks(pair_count)):
            home[s] = home[s] + late[i].astype(f32)
        sends = [block.astype(bf16) for block in home[1:]]
        if c == 0:
            sends, features = lax.optimization_barrier((sends, features))
        total = home[0]
        for s, block in enumerate(sends):
            total = total + sent_round(block, s + 1).astype(f32)
        acts.append(total)

    got_cot, acts[0] = lax.optimization_barrier((got_cot, acts[0]))
    rows = cot_mine.shape[0]
    cot = jnp.where(is_encoder, got_cot[:rows], cot_mine[:, half:])
    gain_rms = jnp.where(is_encoder, got_cot[rows : rows + 1], rms_gain[:, half:])
    slot = lax.broadcasted_iota(jnp.int32, (1, tokens_here), 1) // TOKF
    live_mask = (slot < rotated(counts, tp_index)[:, None]).astype(f32).reshape(-1, 1)
    cot = rotated(cot.reshape(tp_count, tokens_here, half), tp_index).reshape(-1, half)
    scaled = gain_rms.astype(f32) * cot.astype(f32) * live_mask
    scaled = (scaled[:, :first], scaled[:, first:])
    squares = sum(jnp.sum(act * act, axis=1) for act in acts)
    products = sum(jnp.sum(act * part, axis=1) for act, part in zip(acts, scaled))
    sums = jnp.stack([squares, products], axis=1).reshape(tp_count, tokens_here, 2)
    sums = lax.psum(rotated(sums, (tp_count - tp_index) % tp_count), ("grp", "tp"))
    sums = rotated(sums, tp_index).reshape(-1, 2)
    inverse_rms = lax.rsqrt(sums[:, :1] / D + 1e-06)
    fall = inverse_rms**3 * (sums[:, 1:] / D)
    grads = [
        (inverse_rms * part - act * fall).astype(bf16) for act, part in zip(acts, scaled)
    ]

    def gathered_round(block):
        blocks = [block] + [None] * (pair_count - 1)
        for s in range(1, pair_count):
            blocks[s] = sent_round(block, s)
        return jnp.stack(blocks)

    near = gathered_round(grads[0])
    duo = jnp.stack([grads[1], sent_across(grads[1])])
    near, duo = lax.optimization_barrier((near, duo))
    far = sent_across(near)
    duos = gathered_round(duo)
    near, far = (near, duos[:, 0]), (far, duos[:, 1])

    def back(blocks):
        return sum(
            jnp.einsum("prc,kc->prk", block, weight, preferred_element_type=f32)
            for block, weight in zip(blocks, weights)
        )

    terms = [back(near), back(far)]
    terms = jnp.stack(
        [term.reshape(pair_count, tp_count, tokens_here, depth) for term in terms], axis=1
    ).reshape(dp_count, tp_count, tokens_here, depth)
    total = terms[:, 0]
    for s in range(1, tp_count):
        total = total + sent_tp(terms[:, s].astype(bf16), s).astype(f32)
    total = total.astype(bf16)
    total = total.reshape(pair_count, 2, tokens_here, depth)
    middle = pair_count // 2
    summed = [None] * pair_count
    for start, stop in ((middle, pair_count), (0, middle)):
        part = total[start:stop]
        part = part.astype(f32) + passed_along(part, "grp", -1).astype(f32)
        for s in range(start, stop):
            summed[s] = part[s - start].astype(bf16)
    blocks = [summed[0]] + [sent_round(summed[s], s) for s in range(1, pair_count)]
    near = jnp.stack([block[0] for block in blocks])
    far = sent_across(jnp.stack([block[1] for block in blocks]))
    whole = arrange(arrange_last_kernel, "arrange_last", (order,), near, far)
    if depth != CHUNK:
        whole = whole.reshape(-1, CHUNK // depth, tokens_here, depth)
        whole = whole.transpose(0, 2, 1, 3).reshape(-1, tokens_here, CHUNK)

    grad_frames = encoder_backward(flag, w_qkv[0], ln_gain, qkv, probs, norm, inverse, whole)
    return grad_frames[None, None]


def solution(mesh):
    placed = (
        P("grp", ("dp", "tp"), None, None),
        P("dp"),
        P("grp", None, None),
        P("grp", None),
        P("grp", "dp", "tp"),
        P("grp", "tp"),
        P("grp", "dp", "tp"),
    )
    return jax.shard_map(
        per_device,
        mesh=mesh,
        in_specs=placed,
        out_specs=P("grp", ("dp", "tp"), None, None),
        check_vma=False,
    )
```

```python
import jax
import jax.numpy as jnp
from jax import lax
from jax.experimental import pallas as pl
from jax.experimental.pallas import tpu as pltpu
from jax.sharding import PartitionSpec as P

HEADS = 16
HDIM = 80
D = 8192
TOKF = 32
FIRST_PART = 9
GAIN_ROWS = 16
CHUNK = 640
CHUNK_HEADS = CHUNK // HDIM


def head_window(head):
    low, high = head * HDIM, (head + 1) * HDIM
    start, stop = low // 128 * 128, -(-high // 128) * 128
    return start, stop, low - start, high - start


def head_only(block, low, high):
    lane = lax.broadcasted_iota(jnp.int32, block.shape, 1)
    return jnp.where((lane >= low) & (lane < high), block, jnp.zeros_like(block))


def dot(a, b, dims):
    return lax.dot_general(a, b, (dims, ((), ())), preferred_element_type=jnp.float32)


def add_tiles(tiles, block, start):
    for i in range(block.shape[1] // 128):
        tile = start // 128 + i
        part = block[:, i * 128 : (i + 1) * 128]
        tiles[tile] = part if tile not in tiles else tiles[tile] + part


NT = ((1,), (1,))
NN = ((1,), (0,))
TN = ((0,), (0,))


def token_order(length):
    row = lax.broadcasted_iota(jnp.int32, (length, length), 0)
    column = lax.broadcasted_iota(jnp.int32, (length, length), 1)
    tokens = length // 4
    return (row % tokens * 4 + row // tokens == column).astype(jnp.bfloat16)


def weight_copies(w_hbm, w_buf, sems):
    return [
        pltpu.make_async_copy(
            w_hbm.at[:, pl.ds(((i % 3) * 2 + i // 3) * CHUNK, CHUNK)], w_buf.at[i], sems.at[i]
        )
        for i in range(6)
    ]


def encoder_forward_kernel(
    flag_ref,
    x_ref,
    gain_ref,
    w_hbm,
    emb_ref,
    qkv_hbm,
    probs_hbm,
    norm_hbm,
    inv_ref,
    w_buf,
    qkv_ref,
    probs_ref,
    norm_ref,
    work,
    sems,
    out_sems,
):
    @pl.when(flag_ref[0] == 1)
    def _():
        copies = weight_copies(w_hbm, w_buf, sems)
        for copy in copies:
            copy.start()
        outs = []
        x = x_ref[...]
        vis = x.shape[1]
        for half in range(2):
            for kind in range(3):
                i = half * 3 + kind
                copies[i].wait()
                qkv_ref[i] = dot(x, w_buf[i], NN).astype(jnp.bfloat16)
            heads = pl.ds(half * CHUNK_HEADS, CHUNK_HEADS)
            outs.append(
                pltpu.make_async_copy(
                    qkv_ref.at[pl.ds(half * 3, 3)],
                    qkv_hbm.at[pl.ds(half * 3, 3)],
                    out_sems.at[half],
                )
            )
            outs[-1].start()
            tiles = {}
            add_tiles(tiles, x[:, half * CHUNK : (half + 1) * CHUNK].astype(jnp.float32), 0)
            for head in range(CHUNK_HEADS):
                start, stop, low, high = head_window(head)
                query = qkv_ref[half * 3, :, start:stop]
                key = head_only(qkv_ref[half * 3 + 1, :, start:stop], low, high)
                value = head_only(qkv_ref[half * 3 + 2, :, start:stop], low, high)
                scores = dot(query, key, NT) * HDIM ** (-0.5)
                weights = jnp.exp(scores - jnp.max(scores, axis=1, keepdims=True))
                weights = weights / jnp.sum(weights, axis=1, keepdims=True)
                probs_ref[half * CHUNK_HEADS + head] = weights
                add_tiles(tiles, dot(weights.astype(jnp.bfloat16), value, NN), start)
            for tile, part in tiles.items():
                work[half, :, tile * 128 : (tile + 1) * 128] = part
            outs.append(
                pltpu.make_async_copy(probs_ref.at[heads], probs_hbm.at[heads], out_sems.at[2 + half])
            )
            outs[-1].start()
        first, second = work[0], work[1]
        mean = (
            jnp.sum(first, axis=1, keepdims=True) + jnp.sum(second, axis=1, keepdims=True)
        ) / vis
        first, second = first - mean, second - mean
        variance = (
            jnp.sum(first * first, axis=1, keepdims=True)
            + jnp.sum(second * second, axis=1, keepdims=True)
        ) / vis
        inverse = lax.rsqrt(variance + 1e-06)
        inv_ref[...] = inverse
        gain = gain_ref[...].astype(jnp.float32)
        tokens = x.shape[0] // 4
        order = token_order(x.shape[0])
        for half, centred in enumerate((first, second)):
            normal = centred * inverse
            norm_ref[half] = normal
            embedded = (normal * gain[:, half * CHUNK : (half + 1) * CHUNK]).astype(jnp.bfloat16)
            embedded = dot(order, embedded, NN).astype(jnp.bfloat16)
            for j in range(4):
                emb_ref[j * 2 + half] = embedded[j * tokens : (j + 1) * tokens]
        outs.append(pltpu.make_async_copy(norm_ref, norm_hbm, out_sems.at[4]))
        outs[-1].start()
        for copy in outs:
            copy.wait()


def encoder_forward(flag, frame, w_qkv, ln_gain):
    length, vis = frame.shape
    bf16, f32 = jnp.bfloat16, jnp.float32
    vmem = pl.BlockSpec(memory_space=pltpu.VMEM)
    hbm = pl.BlockSpec(memory_space=pltpu.HBM)
    return pl.pallas_call(
        encoder_forward_kernel,
        out_shape=(
            jax.ShapeDtypeStruct((8, length // 4, CHUNK), bf16),
            pltpu.HBM((6, length, CHUNK), bf16),
            pltpu.HBM((HEADS, length, length), f32),
            pltpu.HBM((2, length, CHUNK), f32),
            jax.ShapeDtypeStruct((length, 1), f32),
        ),
        in_specs=[pl.BlockSpec(memory_space=pltpu.SMEM), vmem, vmem, hbm],
        out_specs=(vmem, hbm, hbm, hbm, vmem),
        scratch_shapes=[
            pltpu.VMEM((6, vis, CHUNK), bf16),
            pltpu.VMEM((6, length, CHUNK), bf16),
            pltpu.VMEM((HEADS, length, length), f32),
            pltpu.VMEM((2, length, CHUNK), f32),
            pltpu.VMEM((2, length, CHUNK), f32),
            pltpu.SemaphoreType.DMA((6,)),
            pltpu.SemaphoreType.DMA((5,)),
        ],
        compiler_params=pltpu.CompilerParams(vmem_limit_bytes=24 << 20),
        cost_estimate=pl.CostEstimate(flops=1000, transcendentals=0, bytes_accessed=1000),
        name="encoder_forward",
    )(flag, frame, ln_gain, in_hbm(w_qkv))


def encoder_backward_kernel(
    flag_ref,
    grad_ref,
    gain_ref,
    qkv_ref,
    probs_ref,
    norm_ref,
    inv_ref,
    w_hbm,
    out_ref,
    w_buf,
    work,
    mix,
    sems,
):
    @pl.when(flag_ref[0] == 0)
    def _():
        out_ref[...] = jnp.zeros_like(out_ref)

    @pl.when(flag_ref[0] == 1)
    def _():
        f32, bf16 = jnp.float32, jnp.bfloat16
        copies = weight_copies(w_hbm, w_buf, sems)
        for copy in copies:
            copy.start()
        vis = w_hbm.shape[0]
        tokens = grad_ref.shape[1]
        gain = gain_ref[...].astype(f32)
        order = token_order(4 * tokens)
        for half in range(2):
            grads = jnp.concatenate([grad_ref[j * 2 + half] for j in range(4)], axis=0)
            work[half] = dot(order, grads, TN) * gain[:, half * CHUNK : (half + 1) * CHUNK]
        mean = (
            jnp.sum(work[0], axis=1, keepdims=True) + jnp.sum(work[1], axis=1, keepdims=True)
        ) / vis
        along = (
            jnp.sum(work[0] * norm_ref[0], axis=1, keepdims=True)
            + jnp.sum(work[1] * norm_ref[1], axis=1, keepdims=True)
        ) / vis
        inverse = inv_ref[...]
        for half in range(2):
            work[half] = inverse * (work[half] - mean - norm_ref[half] * along)
        total = jnp.zeros((work.shape[1], vis), f32)
        for half in range(2):
            mixed = [{}, {}, {}]
            for head in range(CHUNK_HEADS):
                start, stop, low, high = head_window(head)
                grad = head_only(work[half, :, start:stop].astype(bf16), low, high)
                query = head_only(qkv_ref[half * 3, :, start:stop], low, high)
                key = head_only(qkv_ref[half * 3 + 1, :, start:stop], low, high)
                value = qkv_ref[half * 3 + 2, :, start:stop]
                probs = probs_ref[half * CHUNK_HEADS + head]
                grad_weights = dot(grad, value, NT)
                inner = jnp.sum(grad_weights * probs, axis=1, keepdims=True)
                scores = (probs * (grad_weights - inner) * HDIM ** (-0.5)).astype(bf16)
                add_tiles(mixed[2], dot(probs.astype(bf16), grad, TN), start)
                add_tiles(mixed[0], dot(scores, key, NN), start)
                add_tiles(mixed[1], dot(scores, query, TN), start)
            for kind in range(3):
                for tile, part in mixed[kind].items():
                    mix[kind, :, tile * 128 : (tile + 1) * 128] = part.astype(bf16)
            for kind in range(3):
                i = half * 3 + kind
                copies[i].wait()
                total = total + dot(mix[kind], w_buf[i], NT)
        for half in range(2):
            columns = slice(half * CHUNK, (half + 1) * CHUNK)
            out_ref[:, columns] = (work[half] + total[:, columns]).astype(bf16)


def encoder_backward(flag, w_qkv, ln_gain, qkv, probs, norm, inverse, grad):
    length, vis = norm.shape[1], w_qkv.shape[0]
    bf16, f32 = jnp.bfloat16, jnp.float32
    vmem = pl.BlockSpec(memory_space=pltpu.VMEM)
    return pl.pallas_call(
        encoder_backward_kernel,
        out_shape=jax.ShapeDtypeStruct((length, vis), bf16),
        in_specs=[pl.BlockSpec(memory_space=pltpu.SMEM)]
        + [vmem] * 6
        + [pl.BlockSpec(memory_space=pltpu.HBM)],
        out_specs=vmem,
        scratch_shapes=[
            pltpu.VMEM((6, vis, CHUNK), bf16),
            pltpu.VMEM((2, length, CHUNK), f32),
            pltpu.VMEM((3, length, CHUNK), bf16),
            pltpu.SemaphoreType.DMA((6,)),
        ],
        compiler_params=pltpu.CompilerParams(vmem_limit_bytes=26 << 20),
        cost_estimate=pl.CostEstimate(flops=1000, transcendentals=0, bytes_accessed=1000),
        name="encoder_backward",
    )(flag, grad, ln_gain, qkv, probs, norm, inverse, in_hbm(w_qkv))


def give_columns_kernel(start, flag_ref, after_ref, w_hbm, out_ref, sem):
    @pl.when(flag_ref[0] == 0)
    def _():
        copy = pltpu.make_async_copy(w_hbm.at[:, pl.ds(start, out_ref.shape[1])], out_ref, sem)
        copy.start()
        copy.wait()


def give_columns(flag, after, matrix, start, size):
    return pl.pallas_call(
        lambda *refs: give_columns_kernel(start, *refs),
        out_shape=jax.ShapeDtypeStruct((matrix.shape[0], size), matrix.dtype),
        in_specs=[
            pl.BlockSpec(memory_space=pltpu.SMEM),
            pl.BlockSpec(memory_space=pl.ANY),
            pl.BlockSpec(memory_space=pltpu.HBM),
        ],
        out_specs=pl.BlockSpec(memory_space=pltpu.VMEM),
        scratch_shapes=[pltpu.SemaphoreType.DMA],
        compiler_params=pltpu.CompilerParams(vmem_limit_bytes=16 << 20),
        cost_estimate=pl.CostEstimate(flops=1000, transcendentals=0, bytes_accessed=1000),
        name="give_columns",
    )(flag, after, in_hbm(matrix))


def give_cotangent_kernel(flag_ref, after_ref, gain_ref, cot_hbm, out_ref, sem):
    @pl.when(flag_ref[0] == 0)
    def _():
        rows, size = cot_hbm.shape[0], out_ref.shape[1]
        copy = pltpu.make_async_copy(
            cot_hbm.at[:, pl.ds(0, size)], out_ref.at[pl.ds(0, rows)], sem
        )
        copy.start()
        out_ref[rows:] = jnp.broadcast_to(gain_ref[:, :size], (GAIN_ROWS, size))
        copy.wait()


def give_cotangent(flag, after, gain, cot, size):
    return pl.pallas_call(
        give_cotangent_kernel,
        out_shape=jax.ShapeDtypeStruct((cot.shape[0] + GAIN_ROWS, size), cot.dtype),
        in_specs=[
            pl.BlockSpec(memory_space=pltpu.SMEM),
            pl.BlockSpec(memory_space=pl.ANY),
            pl.BlockSpec(memory_space=pltpu.VMEM),
            pl.BlockSpec(memory_space=pltpu.HBM),
        ],
        out_specs=pl.BlockSpec(memory_space=pltpu.VMEM),
        scratch_shapes=[pltpu.SemaphoreType.DMA],
        compiler_params=pltpu.CompilerParams(vmem_limit_bytes=16 << 20),
        cost_estimate=pl.CostEstimate(flops=1000, transcendentals=0, bytes_accessed=1000),
        name="give_cotangent",
    )(flag, after, gain, in_hbm(cot))


def in_hbm(array):
    return pltpu.with_memory_space_constraint(array, pltpu.HBM)


def partial_kernel(start, flag_ref, x_ref, got_ref, mine_ref, near_ref, late_ref, *refs):
    *homes, w_ref, sem = refs
    size = w_ref.shape[1]

    @pl.when(flag_ref[0] == 1)
    def _():
        copy = pltpu.make_async_copy(got_ref, w_ref, sem)
        copy.start()
        copy.wait()

    @pl.when(flag_ref[0] == 0)
    def _():
        copy = pltpu.make_async_copy(mine_ref.at[:, pl.ds(start, size)], w_ref, sem)
        copy.start()
        copy.wait()

    pairs, _, rows, depth = x_ref.shape
    weight = w_ref[...]
    away = dot(x_ref[:, 1].reshape(pairs * rows, depth), weight, NN)
    away = [away[s * rows : (s + 1) * rows].astype(near_ref.dtype) for s in range(pairs)]
    for i, s in enumerate(near_blocks(pairs)):
        near_ref[i] = away[s]
    for i, s in enumerate(late_blocks(pairs)):
        late_ref[i] = away[s]
    home = dot(x_ref[:, 0].reshape(pairs * rows, depth), weight, NN)
    for s in range(pairs):
        homes[s][...] = home[s * rows : (s + 1) * rows]


def near_blocks(pairs):
    return list(range(1, pairs // 2 + 1))


def late_blocks(pairs):
    return list(range(pairs // 2 + 1, pairs)) + [0]


def partial_products(flag, features, got, matrix, start):
    pairs, _, rows, depth = features.shape
    size = got.shape[1]
    vmem = pl.BlockSpec(memory_space=pltpu.VMEM)
    half = jax.ShapeDtypeStruct((pairs // 2, rows, size), jnp.bfloat16)
    near, late, *home, weight = pl.pallas_call(
        lambda *refs: partial_kernel(start, *refs),
        out_shape=(half, half)
        + (jax.ShapeDtypeStruct((rows, size), jnp.float32),) * pairs
        + (jax.ShapeDtypeStruct((depth, size), got.dtype),),
        in_specs=[
            pl.BlockSpec(memory_space=pltpu.SMEM),
            vmem,
            pl.BlockSpec(memory_space=pl.ANY),
            pl.BlockSpec(memory_space=pltpu.HBM),
        ],
        out_specs=(vmem,) * (3 + pairs),
        scratch_shapes=[pltpu.SemaphoreType.DMA],
        compiler_params=pltpu.CompilerParams(vmem_limit_bytes=20 << 20),
        cost_estimate=pl.CostEstimate(flops=1000, transcendentals=0, bytes_accessed=1000),
        name="partial_products",
    )(flag, features, in_hbm(got), in_hbm(matrix))
    return near, late, home, weight


def arrange_in_kernel(flag_ref, order_ref, a_ref, b_ref, out_ref):
    keep = flag_ref[0] == 1
    for r in range(out_ref.shape[0]):
        place = order_ref[r]
        out_ref[r] = jnp.where(keep, a_ref[place], b_ref[place])


def arrange_last_kernel(order_ref, near_ref, far_ref, out_ref):
    for s in range(near_ref.shape[0]):
        out_ref[order_ref[2 * s]] = near_ref[s]
        out_ref[order_ref[2 * s + 1]] = far_ref[s]


def arrange(kernel, name, scalars, a, b):
    vmem = pl.BlockSpec(memory_space=pltpu.VMEM)
    return pl.pallas_call(
        kernel,
        out_shape=jax.ShapeDtypeStruct((scalars[-1].shape[0],) + b.shape[1:], b.dtype),
        in_specs=[pl.BlockSpec(memory_space=pltpu.SMEM)] * len(scalars) + [vmem, vmem],
        out_specs=vmem,
        compiler_params=pltpu.CompilerParams(vmem_limit_bytes=32 << 20),
        name=name,
    )(*scalars, a, b)


def passed_along(block, axis, distance):
    devices = range(lax.axis_size(axis))
    route = [(i - distance, i) for i in devices if i - distance in devices]
    return lax.ppermute(block, axis, route)


def rotated(blocks, shift):
    count = blocks.shape[0]
    step = 1
    while step < count:
        turned = jnp.concatenate([blocks[step:], blocks[:step]], axis=0)
        blocks = jnp.where((shift // step) % 2 == 1, turned, blocks)
        step *= 2
    return blocks


def sent_round(block, move):
    count = lax.axis_size("dp")
    return lax.ppermute(block, "dp", [(i, i ^ (2 * move)) for i in range(count)])


def sent_across(block):
    return lax.ppermute(block, "dp", [(i, i ^ 1) for i in range(lax.axis_size("dp"))])


def sent_tp(block, distance):
    count = lax.axis_size("tp")
    return lax.ppermute(block, "tp", [(i, (i + distance) % count) for i in range(count)])


def per_device(frames, counts, w_qkv, ln_gain, w_proj, rms_gain, cotangent):
    f32, bf16 = jnp.float32, jnp.bfloat16
    is_encoder = lax.axis_index("grp") == 0
    flag = is_encoder.astype(jnp.int32).reshape(1)
    dp_count, tp_count = lax.axis_size("dp"), lax.axis_size("tp")
    pair_count = dp_count // 2
    dp_index, tp_index = lax.axis_index("dp"), lax.axis_index("tp")
    relative = jnp.arange(dp_count, dtype=jnp.int32)
    order = dp_index ^ relative

    frame = frames[0, 0]
    tokens_here = frame.shape[0] // 4
    depth = w_proj.shape[1]
    half = w_proj.shape[2] // 2
    first = half * FIRST_PART // 16 // 128 * 128
    sizes = (first, half - first)

    w_mine, cot_mine = w_proj[0], cotangent[0]
    give = [give_columns(flag, flag, w_mine, 0, sizes[0])]
    give.append(give_columns(flag, give[0], w_mine, first, sizes[1]))
    got = [passed_along(block, "grp", -1) for block in give]
    give_cot = give_cotangent(flag, give[1], rms_gain, cot_mine, half)

    embedded, qkv, probs, norm, inverse = encoder_forward(flag, frame, w_qkv[0], ln_gain)

    pieces = embedded
    if depth != CHUNK:
        pieces = embedded.reshape(-1, tokens_here, CHUNK // depth, depth)
        pieces = pieces.transpose(0, 2, 1, 3).reshape(dp_count, tokens_here, depth)
    swapped = lax.all_to_all(pieces, "dp", 0, 0)
    arrived = passed_along(swapped, "grp", 1)
    swapped, give_cot = lax.optimization_barrier((swapped, give_cot))
    got_cot = passed_along(give_cot, "grp", -1)
    features = arrange(arrange_in_kernel, "arrange_in", (flag, order), swapped, arrived)
    features = jnp.concatenate(
        [features] + [sent_tp(features, tp_count - s) for s in range(1, tp_count)], axis=1
    ).reshape(pair_count, 2, tp_count * tokens_here, depth)

    acts, weights = [], []
    for c in range(2):
        near, late, home, weight = partial_products(flag, features, got[c], w_mine, half + c * first)
        weights.append(weight)
        near, late = sent_across(near), sent_across(late)
        for i, s in enumerate(near_blocks(pair_count)):
            home[s] = home[s] + near[i].astype(f32)
        for i, s in enumerate(late_blocks(pair_count)):
            home[s] = home[s] + late[i].astype(f32)
        sends = [block.astype(bf16) for block in home[1:]]
        if c == 0:
            sends, features = lax.optimization_barrier((sends, features))
        total = home[0]
        for s, block in enumerate(sends):
            total = total + sent_round(block, s + 1).astype(f32)
        acts.append(total)

    got_cot, acts[0] = lax.optimization_barrier((got_cot, acts[0]))
    rows = cot_mine.shape[0]
    cot = jnp.where(is_encoder, got_cot[:rows], cot_mine[:, half:])
    gain_rms = jnp.where(is_encoder, got_cot[rows : rows + 1], rms_gain[:, half:])
    slot = lax.broadcasted_iota(jnp.int32, (1, tokens_here), 1) // TOKF
    live_mask = (slot < rotated(counts, tp_index)[:, None]).astype(f32).reshape(-1, 1)
    cot = rotated(cot.reshape(tp_count, tokens_here, half), tp_index).reshape(-1, half)
    scaled = gain_rms.astype(f32) * cot.astype(f32) * live_mask
    scaled = (scaled[:, :first], scaled[:, first:])
    squares = sum(jnp.sum(act * act, axis=1) for act in acts)
    products = sum(jnp.sum(act * part, axis=1) for act, part in zip(acts, scaled))
    sums = jnp.stack([squares, products], axis=1).reshape(tp_count, tokens_here, 2)
    sums = lax.psum(rotated(sums, (tp_count - tp_index) % tp_count), ("grp", "tp"))
    sums = rotated(sums, tp_index).reshape(-1, 2)
    inverse_rms = lax.rsqrt(sums[:, :1] / D + 1e-06)
    fall = inverse_rms**3 * (sums[:, 1:] / D)
    grads = [
        (inverse_rms * part - act * fall).astype(bf16) for act, part in zip(acts, scaled)
    ]

    def gathered_round(block):
        blocks = [block] + [None] * (pair_count - 1)
        for s in range(1, pair_count):
            blocks[s] = sent_round(block, s)
        return jnp.stack(blocks)

    near = gathered_round(grads[0])
    duo = jnp.stack([grads[1], sent_across(grads[1])])
    near, duo = lax.optimization_barrier((near, duo))
    far = sent_across(near)
    duos = gathered_round(duo)
    near, far = (near, duos[:, 0]), (far, duos[:, 1])

    def back(blocks):
        return sum(
            jnp.einsum("prc,kc->prk", block, weight, preferred_element_type=f32)
            for block, weight in zip(blocks, weights)
        )

    terms = [back(near), back(far)]
    terms = jnp.stack(
        [term.reshape(pair_count, tp_count, tokens_here, depth) for term in terms], axis=1
    ).reshape(dp_count, tp_count, tokens_here, depth)
    total = terms[:, 0]
    for s in range(1, tp_count):
        total = total + sent_tp(terms[:, s].astype(bf16), s).astype(f32)
    total = total.astype(bf16)
    total = total.reshape(pair_count, 2, tokens_here, depth)
    middle = pair_count // 2
    summed = [None] * pair_count
    for start, stop in ((0, middle), (middle, pair_count)):
        part = total[start:stop]
        part = part.astype(f32) + passed_along(part, "grp", -1).astype(f32)
        for s in range(start, stop):
            summed[s] = part[s - start].astype(bf16)
    blocks = [summed[0]] + [sent_round(summed[s], s) for s in range(1, pair_count)]
    near = jnp.stack([block[0] for block in blocks])
    far = sent_across(jnp.stack([block[1] for block in blocks]))
    whole = arrange(arrange_last_kernel, "arrange_last", (order,), near, far)
    if depth != CHUNK:
        whole = whole.reshape(-1, CHUNK // depth, tokens_here, depth)
        whole = whole.transpose(0, 2, 1, 3).reshape(-1, tokens_here, CHUNK)

    grad_frames = encoder_backward(flag, w_qkv[0], ln_gain, qkv, probs, norm, inverse, whole)
    return grad_frames[None, None]


def solution(mesh):
    placed = (
        P("grp", ("dp", "tp"), None, None),
        P("dp"),
        P("grp", None, None),
        P("grp", None),
        P("grp", "dp", "tp"),
        P("grp", "tp"),
        P("grp", "dp", "tp"),
    )
    return jax.shard_map(
        per_device,
        mesh=mesh,
        in_specs=placed,
        out_specs=P("grp", ("dp", "tp"), None, None),
        check_vma=False,
    )
```
